32 devices in a mesh: groups: 2 (over x), seq: 16 (over z, y, core).
Axes of the slice: x: 2, y: 2, z: 4, core: 2. Of those that a mesh axis runs over, the one named last changes fastest.
Arguments:
- queries: bfloat16 [16384, 2048], P(('groups', 'seq')), parts along dimension 0, may hold values from -10 to 10
- keys: bfloat16 [16384, 2048], P(('groups', 'seq')), parts along dimension 0, may hold values from -10 to 10
- values: bfloat16 [16384, 2048], P(('groups', 'seq')), parts along dimension 0, may hold values from -6 to 6
- ssd_input: bfloat16 [16384, 2048], P(('groups', 'seq')), parts along dimension 0, may hold values from -6 to 6
- bmat: bfloat16 [16384, 128], P(('groups', 'seq')), parts along dimension 0, may hold values from -0.5 to 0.5
- cmat: bfloat16 [16384, 128], P(('groups', 'seq')), parts along dimension 0, may hold values from -6 to 6
- expo: int32 [16384, 32], P(('groups', 'seq')), parts along dimension 0, may hold values from 1 to 16384
- rate: float32 [32], replicated, may hold values from 1.2207031e-05 to 0.06
- skip: float32 [32], replicated, may hold values from 0.5 to 1.5
Outputs:
- attn_out: bfloat16 [16384, 2048], P(('groups', 'seq')), parts along dimension 0
- normed_recurrence_output: bfloat16 [16384, 2048], P(('groups', 'seq')), parts along dimension 0
The draws below stay inside these ranges and needn't reach their ends.
There are 2 independent parts, one for each index of `groups`. The reference program is written for one: setup_inputs(seed, part) draws one part's arguments, and reference() takes and returns one part's arrays. A program takes and returns all parts, laid end to end along the dimension named above; an argument that names none is the same for every part. Nothing has to cross between parts.
All inputs are finite; a program needn't handle non-finite values.
Results may differ from the reference program's by a relative error of at most 0.0049.
Values may be sent and summed in bfloat16 or wider, within the bound.
A program may use at most 192 MiB of HBM per device.

```python
import math
import jax
import jax.numpy as jnp
from jax import lax

HA = 16
E = 128
W = 2048
HS = 32
P_SIZE = 64
N = 128
Q = 256
DOCUMENT_LENGTH = 8192


def draw_queries(key, part):
    drawn = jnp.clip(1.6 * jax.random.normal(jax.random.fold_in(key, 1), (DOCUMENT_LENGTH, HA * E), jnp.float32), -10.0, 10.0)
    return drawn.astype(jnp.bfloat16)


def draw_keys(key, part):
    drawn = jnp.clip(1.6 * jax.random.normal(jax.random.fold_in(key, 2), (DOCUMENT_LENGTH, HA * E), jnp.float32), -10.0, 10.0)
    return drawn.astype(jnp.bfloat16)


def draw_expo(key, part):
    random_base_key, spike_random_key = jax.random.split(jax.random.fold_in(key, 11))
    base_values_list = jax.random.randint(random_base_key, (DOCUMENT_LENGTH, HS), 1, 4)
    spike_positions = jax.random.randint(spike_random_key, (4,), 0, DOCUMENT_LENGTH)
    spike_row_list = jnp.any(jnp.arange(DOCUMENT_LENGTH)[:, None] == spike_positions[None, :], axis=1)
    return jnp.where(spike_row_list[:, None], 2 * DOCUMENT_LENGTH, base_values_list).astype(jnp.int32)


def draw_rate(key, part):
    slow_key, fast_key, pick_key = jax.random.split(jax.random.fold_in(key, 13), 3)
    slow_rate = jnp.exp(jax.random.uniform(slow_key, (HS,), jnp.float32, math.log(0.1), math.log(0.22))) / DOCUMENT_LENGTH
    fast_rate = jnp.exp(jax.random.uniform(fast_key, (HS,), jnp.float32, math.log(0.02), math.log(0.06)))
    fast_heads = jax.random.uniform(pick_key, (HS,)) < 0.5
    return jnp.where(fast_heads, fast_rate, slow_rate).astype(jnp.float32)


def block_levels(own_key, dims, pieces, low, top_value):
    factor_of = 1.0
    for position, blocks in pieces:
        steps = jax.random.uniform(jax.random.fold_in(jax.random.fold_in(own_key, 6), position), (blocks,), jnp.float32, low / len(pieces), top_value / len(pieces))
        factor_of = factor_of * jnp.repeat(jnp.exp(steps), dims[position] // blocks).reshape((-1,) + (1,) * (len(dims) - 1 - position))
    return factor_of


def centred(stream_key, shape, scale, limit, cuts=(), kind=jnp.bfloat16):
    entries = scale * jax.random.normal(stream_key, shape, jnp.float32)
    if cuts:
        entries = entries * block_levels(stream_key, shape, cuts, -0.22, 0.18)
    return jnp.clip(entries, -limit, limit).astype(kind)


def setup_inputs(seed: int = 0, part: int = 0) -> dict:
    arg_keys = jax.random.split(jax.random.key(seed), 10)
    part_keys = jax.random.split(jax.random.fold_in(arg_keys[9], part), 10)
    queries = draw_queries(jax.random.fold_in(jax.random.fold_in(arg_keys[9], part), 71), part)
    keys = draw_keys(jax.random.fold_in(jax.random.fold_in(arg_keys[9], part), 71), part)
    values = centred(part_keys[2], (DOCUMENT_LENGTH, HA * E), 1.0, 6.0, ((0, 16),))
    ssd_input = centred(part_keys[3], (DOCUMENT_LENGTH, HS * P_SIZE), 1.0, 6.0, ((0, 16),))
    bmat = centred(part_keys[4], (DOCUMENT_LENGTH, N), N ** -0.5, 0.5, ((0, 16),))
    cmat = centred(part_keys[5], (DOCUMENT_LENGTH, N), 1.0, 6.0, ((0, 16),))
    expo = draw_expo(jax.random.fold_in(jax.random.fold_in(arg_keys[9], part), 71), part)
    rate = draw_rate(jax.random.fold_in(arg_keys[9], 71), part)
    skip = jnp.clip(jax.random.uniform(arg_keys[8], (HS,), jnp.float32, 0.5, 1.5), 0.5, 1.5)
    return {"queries": queries, "keys": keys, "values": values, "ssd_input": ssd_input, "bmat": bmat, "cmat": cmat, "expo": expo, "rate": rate, "skip": skip}


def block_local(piece_x, piece_b, piece_c, piece_loga):
    cumulative = jnp.cumsum(piece_loga, axis=0).T
    block_len = cumulative.shape[1]
    lower_mask = jnp.arange(block_len)[:, None] >= jnp.arange(block_len)[None, :]
    log_gaps = cumulative[:, :, None] - cumulative[:, None, :]
    decay_grid = jnp.where(lower_mask[None], jnp.exp(jnp.where(lower_mask[None], log_gaps, 0.0)), 0.0)
    cross_term = jnp.dot(piece_c, piece_b.T, preferred_element_type=jnp.float32)
    inner_term = (cross_term[None] * decay_grid).astype(jnp.bfloat16)
    intra_term = jnp.einsum('hts,shp->thp', inner_term.astype(jnp.float32), piece_x.astype(jnp.float32))
    end_weights = jnp.exp(cumulative[:, -1:] - cumulative)
    weighted = (end_weights.T[:, :, None] * piece_b.astype(jnp.float32)[:, None, :]).astype(jnp.bfloat16)
    local_state = jnp.einsum('shp,shn->hpn', piece_x.astype(jnp.float32), weighted.astype(jnp.float32))
    end_decay = jnp.exp(cumulative[:, -1])
    return (intra_term, cumulative, end_decay, local_state)

def block_output(intra_term, cumulative, piece_x, piece_c, skip, carried):
    inter_term = jnp.einsum('tn,hpn->thp', piece_c.astype(jnp.float32), carried, precision=lax.Precision.HIGHEST)
    mixed = intra_term + inter_term * jnp.exp(cumulative.T)[:, :, None] + skip[None, :, None] * piece_x.astype(jnp.float32)
    inv_rms = lax.rsqrt(lax.optimization_barrier(jnp.mean(mixed * mixed, axis=2, keepdims=True)) + 1e-05)
    return (mixed * inv_rms).astype(jnp.bfloat16).reshape(mixed.shape[0], mixed.shape[1] * mixed.shape[2])

def recurrence_ref(ssd_input, bmat, cmat, expo, rate, skip):
    block_count = DOCUMENT_LENGTH // Q
    all_x = ssd_input.reshape(block_count, Q, HS, P_SIZE)
    all_loga = (-rate[None, :] * expo.astype(jnp.float32)).reshape(block_count, Q, HS)
    all_b = bmat.reshape(block_count, Q, N)
    all_c = cmat.reshape(block_count, Q, N)

    def advance(carried, slices):
        piece_x, piece_b, piece_c, piece_loga = slices
        intra_term, cumulative, end_decay, local_state = block_local(piece_x, piece_b, piece_c, piece_loga)
        result = block_output(intra_term, cumulative, piece_x, piece_c, skip, carried)
        return (end_decay[:, None, None] * carried + local_state, result)
    start_state = jnp.zeros((HS, P_SIZE, N), jnp.float32)
    closing_state, outputs = lax.scan(advance, start_state, (all_x, all_b, all_c, all_loga))
    return outputs.reshape(DOCUMENT_LENGTH, HS * P_SIZE)

def attention_ref(queries, keys, values):
    block_rows = math.gcd(DOCUMENT_LENGTH, 512)
    zero_rows = jnp.zeros((W, HA * E), keys.dtype)
    keys_pad = jnp.concatenate([zero_rows, keys], axis=0)
    values_pad = jnp.concatenate([zero_rows, values], axis=0)

    def one_block(block_index):
        block_start = (block_index * block_rows).astype(jnp.int32)
        query_blk = lax.dynamic_slice_in_dim(queries, block_start, block_rows, 0).reshape(block_rows, HA, E).astype(jnp.float32)
        key_blk = lax.dynamic_slice_in_dim(keys_pad, block_start, block_rows + W, 0).reshape(block_rows + W, HA, E).astype(jnp.float32)
        value_blk = lax.dynamic_slice_in_dim(values_pad, block_start, block_rows + W, 0).reshape(block_rows + W, HA, E).astype(jnp.float32)
        query_pos = block_start + jnp.arange(block_rows, dtype=jnp.int32)
        key_pos = block_start - W + jnp.arange(block_rows + W, dtype=jnp.int32)
        visible = (key_pos[None, :] <= query_pos[:, None]) & (key_pos[None, :] > query_pos[:, None] - W) & (key_pos[None, :] >= 0)
        scores = jnp.einsum('rhe,khe->hrk', query_blk, key_blk) / math.sqrt(E)
        scores = jnp.where(visible[None], scores, -1e+30)
        row_max = lax.optimization_barrier(jnp.max(scores, axis=2, keepdims=True))
        exp_scores = jnp.exp(scores - row_max)
        attn_probs = (exp_scores / lax.optimization_barrier(jnp.sum(exp_scores, axis=2, keepdims=True))).astype(jnp.bfloat16)
        block_out = jnp.einsum('hrk,khe->rhe', attn_probs.astype(jnp.float32), value_blk)
        return block_out.reshape(block_rows, HA * E).astype(jnp.bfloat16)
    outputs = lax.map(one_block, jnp.arange(DOCUMENT_LENGTH // block_rows, dtype=jnp.int32))
    return outputs.reshape(DOCUMENT_LENGTH, HA * E)

def reference(queries, keys, values, ssd_input, bmat, cmat, expo, rate, skip):
    attn_out = attention_ref(queries, keys, values)
    normed_recurrence_output = recurrence_ref(ssd_input, bmat, cmat, expo, rate, skip)
    return (attn_out, normed_recurrence_output)
```

```python
import functools
import math

import jax
import jax.numpy as jnp
from jax import lax
from jax.experimental import pallas as pl
from jax.experimental.pallas import tpu as pltpu
from jax.sharding import PartitionSpec as P

E = 128
Q = 256
LANES = 128
NEG = -1e30
LOG2E = math.log2(math.e)
MESH = pl.DeviceIdType.MESH
Z, Y, A, B = range(4)
BF16 = jnp.bfloat16
F32 = jnp.float32


def dot(a, b):
    return jnp.dot(a, b, preferred_element_type=F32)


def dot_t(a, b):
    return lax.dot_general(a, b, (((1,), (1,)), ((), ())), preferred_element_type=F32)


def iota(shape, axis):
    return lax.broadcasted_iota(jnp.int32, shape, axis)


def split(a):
    high = a.astype(BF16)
    rest = a - high.astype(F32)
    middle = rest.astype(BF16)
    return high, middle, (rest - middle.astype(F32)).astype(BF16)


def table(a):
    parts = split(a)
    rest = jnp.zeros((a.shape[0], LANES - 3 * a.shape[1]), BF16)
    return jnp.concatenate([*parts, rest], axis=1)


def wide(a):
    return jnp.concatenate([a, jnp.zeros((a.shape[0], LANES - a.shape[1]), F32)], axis=1)


def lanes_of(j):
    return pl.ds(pl.multiple_of(j * LANES, LANES), LANES)


def flash(q, tiles, m, l, acc):
    tq = q.shape[0]
    scale = LOG2E / math.sqrt(E)
    for k, v, bias, mask in tiles:
        s = dot_t(q, k) * scale
        if mask is not None:
            row, col = iota((tq, tq), 0), iota((tq, tq), 1)
            s = jnp.where(col <= row if mask == "low" else col > row, s, NEG)
        peak = jnp.max(s, axis=1, keepdims=True)
        if bias is not None:
            peak = peak + bias
        m_new = peak if m is None else jnp.maximum(m, peak)
        shift = m_new if bias is None else m_new - bias
        p = jnp.exp2(s - shift)
        total = jnp.sum(p, axis=1, keepdims=True)
        part = dot(p.astype(BF16), v)
        if m is None:
            l, acc = total, part
        else:
            alpha = jnp.exp2(m - m_new)
            l = l * alpha + total
            acc = acc * alpha + part
        m = m_new
    return m, l, acc


def kernel(
    size, q_in, k_in, v_in, x_in, b_in, c_in, expo_in, rate_ref, skip_ref, attn_ref, rec_ref,
    q_ref, k_ref, v_ref, x_ref, b_ref, c_ref, expo_ref, held, hot, t3, cumt, bt, cross, dec, skx,
    dl, dtab, local, tot, s1, tc, s2, ein, eout, s4out, ec, s5out, carried, mixed, acc_ref, ml_ref,
    load, send, recv, dl_send, dl_recv, s1_send, s1_recv, s5_send, s5_recv, one_send, one_recv,
):
    nz = size // 4
    here = lax.axis_index("seq")
    mine = lax.axis_index("groups")
    z = here // 4
    member = here % 4
    row = member // 2
    core = member % 2
    length, total_cols = q_ref.shape
    x_cols = x_ref.shape[1]
    heads = total_cols // E
    pairs = x_cols // LANES
    head_count = rate_ref.shape[1]
    width = x_cols // head_count
    group = x_cols // 4
    blocks = length // Q
    tq = min(256, length)
    has_z = z > 0
    has_next = z < nz - 1
    has_y = has_z | (row == 1)
    has_b = has_z | (core == 1)

    def beside(d):
        r = 1 - row if d // 2 else row
        c = 1 - core if d % 2 else core
        return (mine, z * 4 + 2 * r + c)

    def beyond(step):
        return (mine, (z + step + nz) % nz * 4 + member)

    def copy(src, dst, sender, receiver, device):
        return pltpu.make_async_remote_copy(
            src_ref=src, dst_ref=dst, send_sem=sender, recv_sem=receiver,
            device_id=device, device_id_type=MESH,
        )

    inputs = (
        (expo_in, expo_ref), (b_in, b_ref), (c_in, c_ref), (x_in, x_ref), (q_in, q_ref),
        (k_in, k_ref), (v_in, v_ref),
    )
    loads = [pltpu.make_async_copy(a, b, load.at[i]) for i, (a, b) in enumerate(inputs)]
    for one in loads[:4]:
        one.start()

    barrier = pltpu.get_barrier_semaphore()
    for d in range(1, 4):
        pl.semaphore_signal(barrier, inc=1, device_id=beside(d), device_id_type=MESH)

    @pl.when(has_z)
    def _():
        pl.semaphore_signal(barrier, inc=1, device_id=beyond(-1), device_id_type=MESH)

    @pl.when(has_next)
    def _():
        pl.semaphore_signal(barrier, inc=1, device_id=beyond(1), device_id_type=MESH)

    pl.semaphore_wait(barrier, 3 + jnp.minimum(z, 1) + jnp.minimum(nz - 1 - z, 1))

    target = {Z: beyond(1), Y: beside(2), A: beside(1), B: beside(1)}

    def send_own(kind, h):
        for part, ref in ((0, k_in), (1, v_in)):
            copy(
                ref.at[:, lanes_of(h)], held.at[kind, h, part], send.at[kind, h], recv.at[kind, h],
                target[kind],
            ).start()

    def whole(kind, h, source):
        return copy(
            held.at[source, h], held.at[kind, h], send.at[kind, h], recv.at[kind, h], target[kind]
        )

    def arrived(kind, h):
        whole(kind, h, kind).wait_recv()

    def sent(kind, h):
        whole(kind, h, kind).wait_send()

    def offer(h):
        @pl.when(has_next)
        def _():
            send_own(Z, h)

        @pl.when(row == 0)
        def _():
            send_own(Y, h)

        @pl.when(core == 0)
        def _():
            send_own(B, h)

    offer(0)
    offer(1)
    for one in loads[4:]:
        one.start()

    def own_dl(d):
        return copy(dl.at[0], dl.at[d], dl_send.at[d], dl_recv.at[d], beside(d))

    def quarter(u, c):
        return pl.ds(pl.multiple_of((2 * u + c) * group, group), group)

    def to_core(u):
        return copy(
            tot.at[:, quarter(u, 1 - core)], s1.at[u], s1_send.at[u], s1_recv.at[u], beside(1)
        )

    def to_row():
        return copy(tc.at[1 - row], s2, one_send.at[0], one_recv.at[0], beside(2))

    def to_next():
        return copy(eout, ein, one_send.at[1], one_recv.at[1], beyond(1))

    def back_row():
        return copy(s4out, ec.at[row], one_send.at[2], one_recv.at[2], beside(2))

    def back_core(u):
        return copy(
            s5out.at[u], carried.at[:, quarter(u, core)], s5_send.at[u], s5_recv.at[u], beside(1)
        )

    ki = iota((LANES, x_cols), 0)
    hi = lax.div(iota((LANES, x_cols), 1), width)
    match = ki == hi
    for p in (1, 2):
        match = match | (ki - p * head_count == hi)
    hot[...] = jnp.where(match, 1.0, 0.0).astype(BF16)

    @pl.when(z == 0)
    def _():
        ein[...] = jnp.zeros_like(ein)

    low = iota((Q, Q), 1) <= iota((Q, Q), 0)
    upto = jnp.where(iota((Q, Q), 0) <= iota((Q, Q), 1), 1.0, 0.0).astype(BF16)
    loads[0].wait()
    rates = wide(rate_ref[...])[0:1, :]
    rates = jnp.broadcast_to(rates, (LANES, LANES)).T[0:head_count, 0:1]
    dlog = None
    for b in range(blocks):
        rs = slice(b * Q, (b + 1) * Q)
        loga = -rates * expo_ref[:, rs].astype(F32)
        sums = sum(dot(part, upto) for part in split(loga))
        cumt[:, rs] = sums
        rest = jnp.zeros((LANES - head_count, Q), F32)
        cum = jnp.concatenate([sums, rest], axis=0).T[:, 0:head_count]
        t3[rs, :] = table(cum)
        last = cum[Q - 1 :, :]
        dlog = last if dlog is None else dlog + last
    dl[0] = jnp.broadcast_to(wide(dlog), dl.shape[1:])
    for d in range(1, 4):
        own_dl(d).start()
    skx[...] = jnp.broadcast_to(dot(table(skip_ref[...]), hot[...]), skx.shape)
    loads[1].wait()
    loads[2].wait()
    bt[...] = b_ref[...].astype(F32).T.astype(BF16)
    for b in range(blocks):
        rs = slice(b * Q, (b + 1) * Q)
        cross[b] = jnp.where(low, dot_t(c_ref[rs, :], b_ref[rs, :]), 0.0)
    loads[3].wait()

    lane = iota((1, LANES), 1)

    def spread(rs, cs):
        return dot(t3[rs, :], hot[:, cs])

    def local_state(j, carry):
        cs = lanes_of(j)
        state = None
        for b in range(blocks):
            rs = slice(b * Q, (b + 1) * Q)
            cum = spread(rs, cs)
            end = cum[Q - 1 :, :]
            xs = x_ref[rs, cs].astype(F32) * jnp.exp(end - cum)
            one = dot(bt[:, rs], xs.astype(BF16))
            grown = jnp.exp(end)
            local[b, :, cs] = one
            dec[b : b + 1, cs] = grown
            state = one if state is None else state * grown + one
        tot[:, cs] = state.astype(BF16)
        return carry

    def intra(j, carry):
        cs = lanes_of(j)
        for b in range(blocks):
            rs = slice(b * Q, (b + 1) * Q)
            cum = spread(rs, cs)
            x = x_ref[rs, cs]
            both = []
            for a in range(2):
                gap = cum[:, a * width : a * width + 1] - cumt[pl.ds(2 * j + a, 1), rs]
                grid = jnp.exp(jnp.minimum(gap, 0.0))
                both.append(dot((cross[b] * grid).astype(BF16), x))
            mixed[rs, cs] = (
                jnp.where(lane < width, both[0], both[1]) + skx[0:1, cs] * x.astype(F32)
            )
        return carry

    same = (iota((LANES, LANES), 0) < width) == (iota((LANES, LANES), 1) < width)
    ones = jnp.where(same, 1.0, 0.0).astype(BF16)

    def finish(j, carry):
        cs = lanes_of(j)
        entry = carried[:, cs].astype(F32)
        for b in range(blocks):
            rs = slice(b * Q, (b + 1) * Q)
            c = c_ref[rs, :]
            high = entry.astype(BF16)
            inter = dot(c, high)
            if b:
                inter = inter + dot(c, (entry - high.astype(F32)).astype(BF16))
            value = mixed[rs, cs] + inter * jnp.exp(spread(rs, cs))
            square = value * value
            big = square.astype(BF16)
            small = (square - big.astype(F32)).astype(BF16)
            mean = (dot(big, ones) + dot(small, ones)) * (1.0 / width)
            rec_ref[rs, cs] = (value * lax.rsqrt(mean + 1e-05)).astype(rec_ref.dtype)
            if b + 1 < blocks:
                entry = entry * dec[b : b + 1, cs] + local[b, :, cs]
        return carry

    def off(seen):
        return jnp.where(seen, 0.0, NEG).astype(F32)

    bias = {Z: off(has_z), Y: off(has_y), A: off(has_y), B: off(has_b)}

    def first_part(h):
        hs = lanes_of(h)
        for r in range(0, length, tq):
            rows = slice(r, r + tq)
            tiles = [(k_ref[rows, hs], v_ref[rows, hs], None, "low")]
            if r > 0:
                tiles.append((k_ref[0:r, hs], v_ref[0:r, hs], None, None))
            tiles.append((held[Z, h, 0, rows, :], held[Z, h, 1, rows, :], bias[Z], "up"))
            if r + tq < length:
                past = slice(r + tq, length)
                tiles.append((held[Z, h, 0, past, :], held[Z, h, 1, past, :], bias[Z], None))
            tiles.append((held[B, h, 0], held[B, h, 1], bias[B], None))
            m, l, acc = flash(q_ref[rows, hs], tiles, None, None, None)
            acc_ref[rows, :] = acc
            ml_ref[0, rows, :] = jnp.broadcast_to(m, acc.shape)
            ml_ref[1, rows, :] = jnp.broadcast_to(l, acc.shape)

    def second_part(h):
        hs = lanes_of(h)
        for r in range(0, length, tq):
            rows = slice(r, r + tq)
            tiles = [(held[n, h, 0], held[n, h, 1], bias[n], None) for n in (Y, A)]
            m, l, acc = flash(
                q_ref[rows, hs], tiles, ml_ref[0, rows, 0:1], ml_ref[1, rows, 0:1], acc_ref[rows, :]
            )
            attn_ref[rows, hs] = (acc / l).astype(attn_ref.dtype)

    @pl.when(z == 0)
    def _():
        def clear(h, carry):
            held[Z, h] = jnp.zeros(held.shape[2:], BF16)

            @pl.when(row == 0)
            def _():
                held[Y, h] = jnp.zeros(held.shape[2:], BF16)
                held[A, h] = jnp.zeros(held.shape[2:], BF16)

            @pl.when(core == 0)
            def _():
                held[B, h] = jnp.zeros(held.shape[2:], BF16)

            return carry

        lax.fori_loop(0, heads, clear, 0)

    def chip_totals():
        for d in range(1, 4):
            own_dl(d).wait_recv()
        which = iota((8, LANES), 0)
        rows = sum(jnp.where(which == d, dl[d], 0.0) for d in range(4))
        dtab[...] = jnp.exp(dot(table(rows[:, :head_count]), hot[...]))
        for u in range(2):
            to_core(u).wait_recv()
            at = quarter(u, core)
            theirs = jnp.where(core == 1, dtab[0:1, at], 1.0)
            ours = jnp.where(core == 1, 1.0, dtab[1:2, at])
            tc[u] = (theirs * s1[u].astype(F32) + ours * tot[:, at].astype(F32)).astype(BF16)
        to_row().start()

    def pass_state():
        to_row().wait_recv()

        @pl.when(has_z)
        def _():
            to_next().wait_recv()

        at = quarter(row, core)
        near = dtab[0:1, at] * dtab[1:2, at]
        far = dtab[2:3, at] * dtab[3:4, at]
        entry = ein[...]
        ours, theirs = tc[row].astype(F32), s2[...].astype(F32)
        quad = jnp.where(row == 1, near, 1.0) * theirs + jnp.where(row == 1, 1.0, far) * ours

        @pl.when(has_next)
        def _():
            eout[...] = near * far * entry + quad
            to_next().start()

        s4out[...] = jnp.where(row == 0, near * entry + ours, entry).astype(BF16)
        back_row().start()
        ec[row] = jnp.where(row == 0, entry, far * entry + theirs).astype(BF16)

    def pass_core():
        back_row().wait_recv()
        for u in range(2):
            at = quarter(u, core)
            entry = ec[u].astype(F32)
            later = jnp.where(core == 0, dtab[0:1, at], dtab[1:2, at]) * entry
            later = later + jnp.where(core == 0, tot[:, at], s1[u]).astype(F32)
            s5out[u] = jnp.where(core == 0, later, entry).astype(BF16)
            back_core(u).start()
            carried[:, at] = jnp.where(core == 0, entry, later).astype(BF16)

    turn = jnp.minimum(3 + 2 * z, 9)
    ready = turn + 3

    def step(j, carry):
        @pl.when(j < heads)
        def _():
            @pl.when(has_z)
            def _():
                arrived(Z, j)

                @pl.when(row == 1)
                def _():
                    whole(Y, j, Z).start()

                @pl.when(core == 1)
                def _():
                    whole(B, j, Z).start()

        @pl.when(j == 1)
        def _():
            chip_totals()

        @pl.when(j == turn)
        def _():
            pass_state()

        @pl.when(j == turn + 2)
        def _():
            pass_core()

        @pl.when(j < heads)
        def _():
            @pl.when(has_next)
            def _():
                sent(Z, j)

            @pl.when(j + 2 < heads)
            def _():
                offer(j + 2)

        @pl.when(j == 0)
        def _():
            lax.fori_loop(0, pairs, local_state, 0)
            for u in range(2):
                to_core(u).start()
            for one in loads[4:]:
                one.wait()

        @pl.when(j >= 2)
        def _():
            @pl.when(has_y)
            def _():
                arrived(A, j - 2)

            second_part(j - 2)

        @pl.when((j >= 1) & (j <= heads))
        def _():
            @pl.when(has_b)
            def _():
                arrived(B, j - 1)

            first_part(j - 1)

        half = (pairs + 7) // 8

        @pl.when((j >= 1) & (j <= 8))
        def _():
            lax.fori_loop((j - 1) * half, jnp.minimum(j * half, pairs), intra, 0)

        fourth = (pairs + 3) // 4

        @pl.when((j >= ready) & (j < ready + 4))
        def _():
            @pl.when(j == ready)
            def _():
                for u in range(2):
                    back_core(u).wait_recv()

            first = (j - ready) * fourth
            lax.fori_loop(first, jnp.minimum(first + fourth, pairs), finish, 0)

        @pl.when((j >= 1) & (j <= heads) & has_y)
        def _():
            arrived(Y, j - 1)
            whole(A, j - 1, Y).start()

        return carry

    lax.fori_loop(0, heads + 2, step, 0)

    for d in range(1, 4):
        own_dl(d).wait_send()
    for u in range(2):
        to_core(u).wait_send()
        back_core(u).wait_send()
    to_row().wait_send()
    back_row().wait_send()

    @pl.when(has_next)
    def _():
        to_next().wait_send()

    def drain(h, carry):
        @pl.when(has_z | (row == 0))
        def _():
            sent(Y, h)

        @pl.when(has_y)
        def _():
            sent(A, h)

        @pl.when(has_z | (core == 0))
        def _():
            sent(B, h)

        return carry

    lax.fori_loop(0, heads, drain, 0)


def on_device(queries, keys, values, ssd_input, bmat, cmat, expo, rate, skip):
    length, total_cols = queries.shape
    size = lax.axis_size("seq")
    head_count = rate.shape[0]
    x_cols = ssd_input.shape[1]
    state = cmat.shape[1]
    heads = total_cols // E
    blocks = length // Q
    group = x_cols // 4
    vmem = pl.BlockSpec(memory_space=pltpu.VMEM)
    anywhere = pl.BlockSpec(memory_space=pl.ANY)
    dma = pltpu.SemaphoreType.DMA
    inputs = (queries, keys, values, ssd_input, bmat, cmat, expo.T)
    big = [pltpu.VMEM(a.shape, a.dtype) for a in inputs]
    return pl.pallas_call(
        functools.partial(kernel, size),
        in_specs=[anywhere] * 7 + [vmem] * 2,
        out_specs=(vmem, vmem),
        out_shape=(
            jax.ShapeDtypeStruct(queries.shape, BF16),
            jax.ShapeDtypeStruct(ssd_input.shape, BF16),
        ),
        scratch_shapes=[
            *big,
            pltpu.VMEM((4, heads, 2, length, E), BF16),
            pltpu.VMEM((LANES, x_cols), BF16),
            pltpu.VMEM((length, LANES), BF16),
            pltpu.VMEM((head_count, length), F32),
            pltpu.VMEM((state, length), BF16),
            pltpu.VMEM((blocks, Q, Q), F32),
            pltpu.VMEM((8, x_cols), F32),
            pltpu.VMEM((8, x_cols), F32),
            pltpu.VMEM((4, 8, LANES), F32),
            pltpu.VMEM((8, x_cols), F32),
            pltpu.VMEM((blocks, state, x_cols), F32),
            pltpu.VMEM((state, x_cols), BF16),
            pltpu.VMEM((2, state, group), BF16),
            pltpu.VMEM((2, state, group), BF16),
            pltpu.VMEM((state, group), BF16),
            pltpu.VMEM((state, group), F32),
            pltpu.VMEM((state, group), F32),
            pltpu.VMEM((state, group), BF16),
            pltpu.VMEM((2, state, group), BF16),
            pltpu.VMEM((2, state, group), BF16),
            pltpu.VMEM((state, x_cols), BF16),
            pltpu.VMEM((length, x_cols), F32),
            pltpu.VMEM((length, E), F32),
            pltpu.VMEM((2, length, E), F32),
            dma((7,)),
            dma((4, heads)),
            dma((4, heads)),
            dma((4,)),
            dma((4,)),
            dma((2,)),
            dma((2,)),
            dma((2,)),
            dma((2,)),
            dma((3,)),
            dma((3,)),
        ],
        compiler_params=pltpu.CompilerParams(
            collective_id=0, has_side_effects=True, vmem_limit_bytes=60 << 20
        ),
        name="attention_and_recurrence",
    )(*inputs, rate[None, :], skip[None, :])


def solution(mesh):
    split_rows = P(("groups", "seq"), None)
    return jax.shard_map(
        on_device,
        mesh=mesh,
        in_specs=(split_rows,) * 7 + (P(), P()),
        out_specs=(split_rows, split_rows),
        check_vma=False,
    )
```

```python
import functools
import math

import jax
import jax.numpy as jnp
from jax import lax
from jax.experimental import pallas as pl
from jax.experimental.pallas import tpu as pltpu
from jax.sharding import PartitionSpec as P

E = 128
Q = 256
LANES = 128
NEG = -1e30
LOG2E = math.log2(math.e)
MESH = pl.DeviceIdType.MESH
Z, Y, A, B = range(4)
BF16 = jnp.bfloat16
F32 = jnp.float32


def dot(a, b):
    return jnp.dot(a, b, preferred_element_type=F32)


def dot_t(a, b):
    return lax.dot_general(a, b, (((1,), (1,)), ((), ())), preferred_element_type=F32)


def iota(shape, axis):
    return lax.broadcasted_iota(jnp.int32, shape, axis)


def split(a):
    high = a.astype(BF16)
    rest = a - high.astype(F32)
    middle = rest.astype(BF16)
    return high, middle, (rest - middle.astype(F32)).astype(BF16)


def table(a):
    parts = split(a)
    rest = jnp.zeros((a.shape[0], LANES - 3 * a.shape[1]), BF16)
    return jnp.concatenate([*parts, rest], axis=1)


def wide(a):
    return jnp.concatenate([a, jnp.zeros((a.shape[0], LANES - a.shape[1]), F32)], axis=1)


def lanes_of(j):
    return pl.ds(pl.multiple_of(j * LANES, LANES), LANES)


def flash(q, tiles, m, l, acc):
    tq = q.shape[0]
    scale = LOG2E / math.sqrt(E)
    for k, v, bias, mask in tiles:
        s = dot_t(q, k) * scale
        if mask is not None:
            row, col = iota((tq, tq), 0), iota((tq, tq), 1)
            s = jnp.where(col <= row if mask == "low" else col > row, s, NEG)
        peak = jnp.max(s, axis=1, keepdims=True)
        if bias is not None:
            peak = peak + bias
        m_new = peak if m is None else jnp.maximum(m, peak)
        shift = m_new if bias is None else m_new - bias
        p = jnp.exp2(s - shift)
        total = jnp.sum(p, axis=1, keepdims=True)
        part = dot(p.astype(BF16), v)
        if m is None:
            l, acc = total, part
        else:
            alpha = jnp.exp2(m - m_new)
            l = l * alpha + total
            acc = acc * alpha + part
        m = m_new
    return m, l, acc


def kernel(
    size, q_in, k_in, v_in, x_in, b_in, c_in, expo_in, rate_in, skip_in, attn_ref, rec_ref,
    q_ref, k_ref, v_ref, x_ref, b_ref, c_ref, expo_ref, rate_ref, skip_ref, held, hot, t3, cumt, bt, cross, dec, skx,
    dl, dtab, local, tot, s1, tc, s2, ein, eout, s4out, ec, s5out, carried, mixed, acc_ref, ml_ref,
    load, send, recv, dl_send, dl_recv, s1_send, s1_recv, s5_send, s5_recv, one_send, one_recv,
):
    nz = size // 4
    here = lax.axis_index("seq")
    mine = lax.axis_index("groups")
    z = here // 4
    member = here % 4
    row = member // 2
    core = member % 2
    length, total_cols = q_ref.shape
    x_cols = x_ref.shape[1]
    heads = total_cols // E
    pairs = x_cols // LANES
    head_count = rate_ref.shape[1]
    width = x_cols // head_count
    group = x_cols // 4
    blocks = length // Q
    tq = min(256, length)
    has_z = z > 0
    has_next = z < nz - 1
    has_y = has_z | (row == 1)
    has_b = has_z | (core == 1)

    def beside(d):
        r = 1 - row if d // 2 else row
        c = 1 - core if d % 2 else core
        return (mine, z * 4 + 2 * r + c)

    def beyond(step):
        return (mine, (z + step + nz) % nz * 4 + member)

    def copy(src, dst, sender, receiver, device):
        return pltpu.make_async_remote_copy(
            src_ref=src, dst_ref=dst, send_sem=sender, recv_sem=receiver,
            device_id=device, device_id_type=MESH,
        )

    inputs = (
        (rate_in, rate_ref), (expo_in, expo_ref), (skip_in, skip_ref), (b_in, b_ref), (c_in, c_ref),
        (x_in, x_ref), (q_in, q_ref), (k_in, k_ref), (v_in, v_ref),
    )
    loads = [pltpu.make_async_copy(a, b, load.at[i]) for i, (a, b) in enumerate(inputs)]
    for one in loads[:6]:
        one.start()

    barrier = pltpu.get_barrier_semaphore()
    for d in range(1, 4):
        pl.semaphore_signal(barrier, inc=1, device_id=beside(d), device_id_type=MESH)

    @pl.when(has_z)
    def _():
        pl.semaphore_signal(barrier, inc=1, device_id=beyond(-1), device_id_type=MESH)

    @pl.when(has_next)
    def _():
        pl.semaphore_signal(barrier, inc=1, device_id=beyond(1), device_id_type=MESH)

    pl.semaphore_wait(barrier, 3 + jnp.minimum(z, 1) + jnp.minimum(nz - 1 - z, 1))

    target = {Z: beyond(1), Y: beside(2), A: beside(1), B: beside(1)}

    def send_own(kind, h):
        for part, ref in ((0, k_in), (1, v_in)):
            copy(
                ref.at[:, lanes_of(h)], held.at[kind, h, part], send.at[kind, h], recv.at[kind, h],
                target[kind],
            ).start()

    def whole(kind, h, source):
        return copy(
            held.at[source, h], held.at[kind, h], send.at[kind, h], recv.at[kind, h], target[kind]
        )

    def arrived(kind, h):
        whole(kind, h, kind).wait_recv()

    def sent(kind, h):
        whole(kind, h, kind).wait_send()

    def offer(h):
        @pl.when(has_next)
        def _():
            send_own(Z, h)

        @pl.when(row == 0)
        def _():
            send_own(Y, h)

        @pl.when(core == 0)
        def _():
            send_own(B, h)

    offer(0)
    offer(1)
    for one in loads[6:]:
        one.start()

    def own_dl(d):
        return copy(dl.at[0], dl.at[d], dl_send.at[d], dl_recv.at[d], beside(d))

    def quarter(u, c):
        return pl.ds(pl.multiple_of((2 * u + c) * group, group), group)

    def to_core(u):
        return copy(
            tot.at[:, quarter(u, 1 - core)], s1.at[u], s1_send.at[u], s1_recv.at[u], beside(1)
        )

    def to_row():
        return copy(tc.at[1 - row], s2, one_send.at[0], one_recv.at[0], beside(2))

    def to_next():
        return copy(eout, ein, one_send.at[1], one_recv.at[1], beyond(1))

    def back_row():
        return copy(s4out, ec.at[row], one_send.at[2], one_recv.at[2], beside(2))

    def back_core(u):
        return copy(
            s5out.at[u], carried.at[:, quarter(u, core)], s5_send.at[u], s5_recv.at[u], beside(1)
        )

    ki = iota((LANES, x_cols), 0)
    hi = lax.div(iota((LANES, x_cols), 1), width)
    match = ki == hi
    for p in (1, 2):
        match = match | (ki - p * head_count == hi)
    hot[...] = jnp.where(match, 1.0, 0.0).astype(BF16)

    @pl.when(z == 0)
    def _():
        ein[...] = jnp.zeros_like(ein)

    low = iota((Q, Q), 1) <= iota((Q, Q), 0)
    upto = jnp.where(iota((Q, Q), 0) <= iota((Q, Q), 1), 1.0, 0.0).astype(BF16)
    loads[0].wait()
    loads[1].wait()
    rates = wide(rate_ref[...])[0:1, :]
    rates = jnp.broadcast_to(rates, (LANES, LANES)).T[0:head_count, 0:1]
    dlog = None
    for b in range(blocks):
        rs = slice(b * Q, (b + 1) * Q)
        loga = -rates * expo_ref[:, rs].astype(F32)
        sums = sum(dot(part, upto) for part in split(loga))
        cumt[:, rs] = sums
        rest = jnp.zeros((LANES - head_count, Q), F32)
        cum = jnp.concatenate([sums, rest], axis=0).T[:, 0:head_count]
        t3[rs, :] = table(cum)
        last = cum[Q - 1 :, :]
        dlog = last if dlog is None else dlog + last
    dl[0] = jnp.broadcast_to(wide(dlog), dl.shape[1:])
    for d in range(1, 4):
        own_dl(d).start()
    loads[2].wait()
    skx[...] = jnp.broadcast_to(dot(table(skip_ref[...]), hot[...]), skx.shape)
    loads[3].wait()
    loads[4].wait()
    bt[...] = b_ref[...].astype(F32).T.astype(BF16)
    for b in range(blocks):
        rs = slice(b * Q, (b + 1) * Q)
        cross[b] = jnp.where(low, dot_t(c_ref[rs, :], b_ref[rs, :]), 0.0)
    loads[5].wait()

    lane = iota((1, LANES), 1)

    def spread(rs, cs):
        return dot(t3[rs, :], hot[:, cs])

    def local_state(j, carry):
        cs = lanes_of(j)
        state = None
        for b in range(blocks):
            rs = slice(b * Q, (b + 1) * Q)
            cum = spread(rs, cs)
            end = cum[Q - 1 :, :]
            xs = x_ref[rs, cs].astype(F32) * jnp.exp(end - cum)
            one = dot(bt[:, rs], xs.astype(BF16))
            grown = jnp.exp(end)
            local[b, :, cs] = one
            dec[b : b + 1, cs] = grown
            state = one if state is None else state * grown + one
        tot[:, cs] = state.astype(BF16)
        return carry

    def intra(j, carry):
        cs = lanes_of(j)
        for b in range(blocks):
            rs = slice(b * Q, (b + 1) * Q)
            cum = spread(rs, cs)
            x = x_ref[rs, cs]
            both = []
            for a in range(2):
                gap = cum[:, a * width : a * width + 1] - cumt[pl.ds(2 * j + a, 1), rs]
                grid = jnp.exp(jnp.minimum(gap, 0.0))
                both.append(dot((cross[b] * grid).astype(BF16), x))
            mixed[rs, cs] = (
                jnp.where(lane < width, both[0], both[1]) + skx[0:1, cs] * x.astype(F32)
            )
        return carry

    same = (iota((LANES, LANES), 0) < width) == (iota((LANES, LANES), 1) < width)
    ones = jnp.where(same, 1.0, 0.0).astype(BF16)

    def finish(j, carry):
        cs = lanes_of(j)
        entry = carried[:, cs].astype(F32)
        for b in range(blocks):
            rs = slice(b * Q, (b + 1) * Q)
            c = c_ref[rs, :]
            high = entry.astype(BF16)
            inter = dot(c, high)
            if b:
                inter = inter + dot(c, (entry - high.astype(F32)).astype(BF16))
            value = mixed[rs, cs] + inter * jnp.exp(spread(rs, cs))
            square = value * value
            big = square.astype(BF16)
            small = (square - big.astype(F32)).astype(BF16)
            mean = (dot(big, ones) + dot(small, ones)) * (1.0 / width)
            rec_ref[rs, cs] = (value * lax.rsqrt(mean + 1e-05)).astype(rec_ref.dtype)
            if b + 1 < blocks:
                entry = entry * dec[b : b + 1, cs] + local[b, :, cs]
        return carry

    def off(seen):
        return jnp.where(seen, 0.0, NEG).astype(F32)

    bias = {Z: off(has_z), Y: off(has_y), A: off(has_y), B: off(has_b)}

    def first_part(h):
        hs = lanes_of(h)
        for r in range(0, length, tq):
            rows = slice(r, r + tq)
            tiles = [(k_ref[rows, hs], v_ref[rows, hs], None, "low")]
            if r > 0:
                tiles.append((k_ref[0:r, hs], v_ref[0:r, hs], None, None))
            tiles.append((held[Z, h, 0, rows, :], held[Z, h, 1, rows, :], bias[Z], "up"))
            if r + tq < length:
                past = slice(r + tq, length)
                tiles.append((held[Z, h, 0, past, :], held[Z, h, 1, past, :], bias[Z], None))
            tiles.append((held[B, h, 0], held[B, h, 1], bias[B], None))
            m, l, acc = flash(q_ref[rows, hs], tiles, None, None, None)
            acc_ref[rows, :] = acc
            ml_ref[0, rows, :] = jnp.broadcast_to(m, acc.shape)
            ml_ref[1, rows, :] = jnp.broadcast_to(l, acc.shape)

    def second_part(h):
        hs = lanes_of(h)
        for r in range(0, length, tq):
            rows = slice(r, r + tq)
            tiles = [(held[n, h, 0], held[n, h, 1], bias[n], None) for n in (Y, A)]
            m, l, acc = flash(
                q_ref[rows, hs], tiles, ml_ref[0, rows, 0:1], ml_ref[1, rows, 0:1], acc_ref[rows, :]
            )
            attn_ref[rows, hs] = (acc / l).astype(attn_ref.dtype)

    @pl.when(z == 0)
    def _():
        def clear(h, carry):
            held[Z, h] = jnp.zeros(held.shape[2:], BF16)

            @pl.when(row == 0)
            def _():
                held[Y, h] = jnp.zeros(held.shape[2:], BF16)
                held[A, h] = jnp.zeros(held.shape[2:], BF16)

            @pl.when(core == 0)
            def _():
                held[B, h] = jnp.zeros(held.shape[2:], BF16)

            return carry

        lax.fori_loop(0, heads, clear, 0)

    def chip_totals():
        for d in range(1, 4):
            own_dl(d).wait_recv()
        which = iota((8, LANES), 0)
        rows = sum(jnp.where(which == d, dl[d], 0.0) for d in range(4))
        dtab[...] = jnp.exp(dot(table(rows[:, :head_count]), hot[...]))
        for u in range(2):
            to_core(u).wait_recv()
            at = quarter(u, core)
            theirs = jnp.where(core == 1, dtab[0:1, at], 1.0)
            ours = jnp.where(core == 1, 1.0, dtab[1:2, at])
            tc[u] = (theirs * s1[u].astype(F32) + ours * tot[:, at].astype(F32)).astype(BF16)
        to_row().start()

    def pass_state():
        to_row().wait_recv()

        @pl.when(has_z)
        def _():
            to_next().wait_recv()

        at = quarter(row, core)
        near = dtab[0:1, at] * dtab[1:2, at]
        far = dtab[2:3, at] * dtab[3:4, at]
        entry = ein[...]
        ours, theirs = tc[row].astype(F32), s2[...].astype(F32)
        quad = jnp.where(row == 1, near, 1.0) * theirs + jnp.where(row == 1, 1.0, far) * ours

        @pl.when(has_next)
        def _():
            eout[...] = near * far * entry + quad
            to_next().start()

        s4out[...] = jnp.where(row == 0, near * entry + ours, entry).astype(BF16)
        back_row().start()
        ec[row] = jnp.where(row == 0, entry, far * entry + theirs).astype(BF16)

    def pass_core():
        back_row().wait_recv()
        for u in range(2):
            at = quarter(u, core)
            entry = ec[u].astype(F32)
            later = jnp.where(core == 0, dtab[0:1, at], dtab[1:2, at]) * entry
            later = later + jnp.where(core == 0, tot[:, at], s1[u]).astype(F32)
            s5out[u] = jnp.where(core == 0, later, entry).astype(BF16)
            back_core(u).start()
            carried[:, at] = jnp.where(core == 0, entry, later).astype(BF16)

    turn = jnp.minimum(3 + 2 * z, 9)
    ready = turn + 3

    def step(j, carry):
        @pl.when(j < heads)
        def _():
            @pl.when(has_z)
            def _():
                arrived(Z, j)

                @pl.when(row == 1)
                def _():
                    whole(Y, j, Z).start()

                @pl.when(core == 1)
                def _():
                    whole(B, j, Z).start()

        @pl.when(j == 1)
        def _():
            chip_totals()

        @pl.when(j == turn)
        def _():
            pass_state()

        @pl.when(j == turn + 2)
        def _():
            pass_core()

        @pl.when(j < heads)
        def _():
            @pl.when(has_next)
            def _():
                sent(Z, j)

            @pl.when(j + 2 < heads)
            def _():
                offer(j + 2)

        @pl.when(j == 0)
        def _():
            lax.fori_loop(0, pairs, local_state, 0, unroll=4)
            for u in range(2):
                to_core(u).start()
            for one in loads[6:]:
                one.wait()

        @pl.when(j >= 2)
        def _():
            @pl.when(has_y)
            def _():
                arrived(A, j - 2)

            second_part(j - 2)

        @pl.when((j >= 1) & (j <= heads) & has_y)
        def _():
            arrived(Y, j - 1)
            whole(A, j - 1, Y).start()

        @pl.when((j >= 1) & (j <= heads))
        def _():
            @pl.when(has_b)
            def _():
                arrived(B, j - 1)

            first_part(j - 1)

        @pl.when((j >= 1) & (j <= pairs // 2))
        def _():
            for n in range(2):
                intra(2 * (j - 1) + n, 0)

        fourth = pairs // 4

        @pl.when((j >= ready) & (j < ready + 4))
        def _():
            @pl.when(j == ready)
            def _():
                for u in range(2):
                    back_core(u).wait_recv()

            for n in range(fourth):
                finish((j - ready) * fourth + n, 0)

        return carry

    lax.fori_loop(0, heads + 2, step, 0)

    for d in range(1, 4):
        own_dl(d).wait_send()
    for u in range(2):
        to_core(u).wait_send()
        back_core(u).wait_send()
    to_row().wait_send()
    back_row().wait_send()

    @pl.when(has_next)
    def _():
        to_next().wait_send()

    def drain(h, carry):
        @pl.when(has_z | (row == 0))
        def _():
            sent(Y, h)

        @pl.when(has_y)
        def _():
            sent(A, h)

        @pl.when(has_z | (core == 0))
        def _():
            sent(B, h)

        return carry

    lax.fori_loop(0, heads, drain, 0)


def on_device(queries, keys, values, ssd_input, bmat, cmat, expo, rate, skip):
    length, total_cols = queries.shape
    size = lax.axis_size("seq")
    head_count = rate.shape[0]
    x_cols = ssd_input.shape[1]
    state = cmat.shape[1]
    heads = total_cols // E
    blocks = length // Q
    group = x_cols // 4
    vmem = pl.BlockSpec(memory_space=pltpu.VMEM)
    dma = pltpu.SemaphoreType.DMA
    inputs = (
        queries, keys, values, ssd_input, bmat, cmat, expo.T, rate[None, :], skip[None, :]
    )
    big = [pltpu.VMEM(a.shape, a.dtype) for a in inputs]
    return pl.pallas_call(
        functools.partial(kernel, size),
        in_specs=[pl.BlockSpec(memory_space=pltpu.HBM)] * len(inputs),
        out_specs=(vmem, vmem),
        out_shape=(
            jax.ShapeDtypeStruct(queries.shape, BF16),
            jax.ShapeDtypeStruct(ssd_input.shape, BF16),
        ),
        scratch_shapes=[
            *big,
            pltpu.VMEM((4, heads, 2, length, E), BF16),
            pltpu.VMEM((LANES, x_cols), BF16),
            pltpu.VMEM((length, LANES), BF16),
            pltpu.VMEM((head_count, length), F32),
            pltpu.VMEM((state, length), BF16),
            pltpu.VMEM((blocks, Q, Q), F32),
            pltpu.VMEM((8, x_cols), F32),
            pltpu.VMEM((8, x_cols), F32),
            pltpu.VMEM((4, 8, LANES), F32),
            pltpu.VMEM((8, x_cols), F32),
            pltpu.VMEM((blocks, state, x_cols), F32),
            pltpu.VMEM((state, x_cols), BF16),
            pltpu.VMEM((2, state, group), BF16),
            pltpu.VMEM((2, state, group), BF16),
            pltpu.VMEM((state, group), BF16),
            pltpu.VMEM((state, group), F32),
            pltpu.VMEM((state, group), F32),
            pltpu.VMEM((state, group), BF16),
            pltpu.VMEM((2, state, group), BF16),
            pltpu.VMEM((2, state, group), BF16),
            pltpu.VMEM((state, x_cols), BF16),
            pltpu.VMEM((length, x_cols), F32),
            pltpu.VMEM((length, E), F32),
            pltpu.VMEM((2, length, E), F32),
            dma((9,)),
            dma((4, heads)),
            dma((4, heads)),
            dma((4,)),
            dma((4,)),
            dma((2,)),
            dma((2,)),
            dma((2,)),
            dma((2,)),
            dma((3,)),
            dma((3,)),
        ],
        compiler_params=pltpu.CompilerParams(
            collective_id=0, has_side_effects=True, vmem_limit_bytes=48 << 20
        ),
        name="attention_and_recurrence",
    )(*(pltpu.with_memory_space_constraint(a, pltpu.HBM) for a in inputs))


def solution(mesh):
    split_rows = P(("groups", "seq"), None)
    return jax.shard_map(
        on_device,
        mesh=mesh,
        in_specs=(split_rows,) * 7 + (P(), P()),
        out_specs=(split_rows, split_rows),
        check_vma=False,
    )
```

```python
import functools
import math

import jax
import jax.numpy as jnp
from jax import lax
from jax.experimental import pallas as pl
from jax.experimental.pallas import tpu as pltpu
from jax.sharding import PartitionSpec as P

E = 128
Q = 256
LANES = 128
NEG = -1e30
LOG2E = math.log2(math.e)
MESH = pl.DeviceIdType.MESH
Z, Y, A, B = range(4)
BF16 = jnp.bfloat16
F32 = jnp.float32


def dot(a, b):
    return jnp.dot(a, b, preferred_element_type=F32)


def dot_t(a, b):
    return lax.dot_general(a, b, (((1,), (1,)), ((), ())), preferred_element_type=F32)


def iota(shape, axis):
    return lax.broadcasted_iota(jnp.int32, shape, axis)


def split(a):
    high = a.astype(BF16)
    rest = a - high.astype(F32)
    middle = rest.astype(BF16)
    return high, middle, (rest - middle.astype(F32)).astype(BF16)


def table(a):
    parts = split(a)
    rest = jnp.zeros((a.shape[0], LANES - 3 * a.shape[1]), BF16)
    return jnp.concatenate([*parts, rest], axis=1)


def wide(a):
    return jnp.concatenate([a, jnp.zeros((a.shape[0], LANES - a.shape[1]), F32)], axis=1)


def lanes_of(j):
    return pl.ds(pl.multiple_of(j * LANES, LANES), LANES)


def flash(q, tiles, m, l, acc):
    tq = q.shape[0]
    scale = LOG2E / math.sqrt(E)
    for k, v, bias, mask in tiles:
        s = dot_t(q, k) * scale
        if mask is not None:
            row, col = iota((tq, tq), 0), iota((tq, tq), 1)
            s = jnp.where(col <= row if mask == "low" else col > row, s, NEG)
        peak = jnp.max(s, axis=1, keepdims=True)
        if bias is not None:
            peak = peak + bias
        m_new = peak if m is None else jnp.maximum(m, peak)
        shift = m_new if bias is None else m_new - bias
        p = jnp.exp2(s - shift)
        total = jnp.sum(p, axis=1, keepdims=True)
        part = dot(p.astype(BF16), v)
        if m is None:
            l, acc = total, part
        else:
            alpha = jnp.exp2(m - m_new)
            l = l * alpha + total
            acc = acc * alpha + part
        m = m_new
    return m, l, acc


def kernel(
    size, q_in, k_in, v_in, x_in, b_in, c_in, expo_in, rate_in, skip_in, attn_ref, rec_ref,
    q_ref, k_ref, v_ref, x_ref, b_ref, c_ref, expo_ref, rate_ref, skip_ref, held, hot, t3, cumt, bt, cross, dec, skx,
    dl, dtab, local, tot, s1, tc, s2, ein, eout, s4out, ec, s5out, carried, mixed, acc_ref, ml_ref,
    load, z_send, z_recv, edge_recv, side_send, side_recv, dl_send, dl_recv, s1_send, s1_recv, s5_send, s5_recv, one_send, one_recv,
):
    nz = size // 4
    here = lax.axis_index("seq")
    mine = lax.axis_index("groups")
    z = here // 4
    member = here % 4
    row = member // 2
    core = member % 2
    length, total_cols = q_ref.shape
    x_cols = x_ref.shape[1]
    heads = total_cols // E
    pairs = x_cols // LANES
    head_count = rate_ref.shape[1]
    width = x_cols // head_count
    group = x_cols // 4
    blocks = length // Q
    tq = min(256, length)
    has_z = z > 0
    has_next = z < nz - 1
    has_y = has_z | (row == 1)
    has_b = has_z | (core == 1)

    def beside(d):
        r = 1 - row if d // 2 else row
        c = 1 - core if d % 2 else core
        return (mine, z * 4 + 2 * r + c)

    def beyond(step):
        return (mine, (z + step + nz) % nz * 4 + member)

    def copy(src, dst, sender, receiver, device):
        return pltpu.make_async_remote_copy(
            src_ref=src, dst_ref=dst, send_sem=sender, recv_sem=receiver,
            device_id=device, device_id_type=MESH,
        )

    inputs = (
        (rate_in, rate_ref), (expo_in, expo_ref), (skip_in, skip_ref), (b_in, b_ref), (c_in, c_ref),
        (x_in, x_ref), (q_in, q_ref), (k_in, k_ref), (v_in, v_ref),
    )
    loads = [pltpu.make_async_copy(a, b, load.at[i]) for i, (a, b) in enumerate(inputs)]
    for one in loads[:6]:
        one.start()

    barrier = pltpu.get_barrier_semaphore()
    for d in range(1, 4):
        pl.semaphore_signal(barrier, inc=1, device_id=beside(d), device_id_type=MESH)

    @pl.when(has_z)
    def _():
        pl.semaphore_signal(barrier, inc=1, device_id=beyond(-1), device_id_type=MESH)

    @pl.when(has_next)
    def _():
        pl.semaphore_signal(barrier, inc=1, device_id=beyond(1), device_id_type=MESH)

    pl.semaphore_wait(barrier, 3 + jnp.minimum(z, 1) + jnp.minimum(nz - 1 - z, 1))

    target = {Z: beyond(1), Y: beside(2), A: beside(1), B: beside(1)}

    def side(kind, h, source):
        return copy(
            held.at[source, h], held.at[kind, h], side_send.at[kind - 1], side_recv.at[kind - 1, h],
            target[kind],
        )

    def arrived(kind, h):
        side(kind, h, kind).wait_recv()

    def all_sent(kind):
        copy(
            held.at[kind], held.at[kind], side_send.at[kind - 1], side_recv.at[kind - 1, 0],
            target[kind],
        ).wait_send()

    piece = length // 4
    halves = [(part, slice(0, length)) for part in range(2)]
    pieces = [(part, slice(i * piece, (i + 1) * piece)) for part in range(2) for i in range(4)]

    def z_copy(h, n, cut, arrival):
        part, rows = cut[n]
        return copy(
            (k_in, v_in)[part].at[rows, lanes_of(h)], held.at[Z, h, part, rows], z_send.at[h],
            arrival(n), target[Z],
        )

    def z_relay(h, n, cut, kind):
        part, rows = cut[n]
        return copy(
            held.at[Z, h, part, rows], held.at[kind, h, part, rows], side_send.at[kind - 1],
            side_recv.at[kind - 1, h], target[kind],
        )

    def first_sems(n):
        return edge_recv.at[0, n]

    def last_sems(n):
        return edge_recv.at[1, n]

    def z_arrived(h, n, cut, arrival):
        @pl.when(has_z)
        def _():
            z_copy(h, n, cut, arrival).wait_recv()

            @pl.when(row == 1)
            def _():
                z_relay(h, n, cut, Y).start()

            @pl.when(core == 1)
            def _():
                z_relay(h, n, cut, B).start()

    def z_sent(h):
        copy(
            held.at[Z, h], held.at[Z, h], z_send.at[h], z_recv.at[h, 0], target[Z]
        ).wait_send()

    def z_offer(h, cut, arrival):
        @pl.when(has_next)
        def _():
            for n in range(len(cut)):
                z_copy(h, n, cut, arrival).start()

    def side_offer(h):
        def send_own(kind):
            for part, ref in ((0, k_in), (1, v_in)):
                copy(
                    ref.at[:, lanes_of(h)], held.at[kind, h, part], side_send.at[kind - 1],
                    side_recv.at[kind - 1, h], target[kind],
                ).start()

        @pl.when(row == 0)
        def _():
            send_own(Y)

        @pl.when(core == 0)
        def _():
            send_own(B)

    def z_sems(h):
        return lambda n: z_recv.at[h, n]

    z_offer(0, pieces, first_sems)
    side_offer(0)
    z_offer(1, halves, z_sems(1))
    side_offer(1)
    for one in loads[6:]:
        one.start()

    def own_dl(d):
        return copy(dl.at[0], dl.at[d], dl_send.at[d], dl_recv.at[d], beside(d))

    def quarter(u, c):
        return pl.ds(pl.multiple_of((2 * u + c) * group, group), group)

    def to_core(u):
        return copy(
            tot.at[:, quarter(u, 1 - core)], s1.at[u], s1_send.at[u], s1_recv.at[u], beside(1)
        )

    def to_row():
        return copy(tc.at[1 - row], s2, one_send.at[0], one_recv.at[0], beside(2))

    def to_next():
        return copy(eout, ein, one_send.at[1], one_recv.at[1], beyond(1))

    def back_row():
        return copy(s4out, ec.at[row], one_send.at[2], one_recv.at[2], beside(2))

    def back_core(u):
        return copy(
            s5out.at[u], carried.at[:, quarter(u, core)], s5_send.at[u], s5_recv.at[u], beside(1)
        )

    ki = iota((LANES, x_cols), 0)
    hi = lax.div(iota((LANES, x_cols), 1), width)
    match = ki == hi
    for p in (1, 2):
        match = match | (ki - p * head_count == hi)
    hot[...] = jnp.where(match, 1.0, 0.0).astype(BF16)

    @pl.when(z == 0)
    def _():
        ein[...] = jnp.zeros_like(ein)

    low = iota((Q, Q), 1) <= iota((Q, Q), 0)
    upto = jnp.where(iota((Q, Q), 0) <= iota((Q, Q), 1), 1.0, 0.0).astype(BF16)
    loads[0].wait()
    loads[1].wait()
    rates = wide(rate_ref[...])[0:1, :]
    rates = jnp.broadcast_to(rates, (LANES, LANES)).T[0:head_count, 0:1]
    dlog = None
    for b in range(blocks):
        rs = slice(b * Q, (b + 1) * Q)
        loga = -rates * expo_ref[:, rs].astype(F32)
        sums = sum(dot(part, upto) for part in split(loga))
        cumt[:, rs] = sums
        rest = jnp.zeros((LANES - head_count, Q), F32)
        cum = jnp.concatenate([sums, rest], axis=0).T[:, 0:head_count]
        t3[rs, :] = table(cum)
        last = cum[Q - 1 :, :]
        dlog = last if dlog is None else dlog + last
    dl[0] = jnp.broadcast_to(wide(dlog), dl.shape[1:])
    for d in range(1, 4):
        own_dl(d).start()
    loads[2].wait()
    skx[...] = jnp.broadcast_to(dot(table(skip_ref[...]), hot[...]), skx.shape)
    loads[3].wait()
    loads[4].wait()
    bt[...] = b_ref[...].astype(F32).T.astype(BF16)
    for b in range(blocks):
        rs = slice(b * Q, (b + 1) * Q)
        cross[b] = jnp.where(low, dot_t(c_ref[rs, :], b_ref[rs, :]), 0.0)
    loads[5].wait()

    lane = iota((1, LANES), 1)

    def spread(rs, cs):
        return dot(t3[rs, :], hot[:, cs])

    def local_state(j, carry):
        cs = lanes_of(j)
        state = None
        for b in range(blocks):
            rs = slice(b * Q, (b + 1) * Q)
            cum = spread(rs, cs)
            end = cum[Q - 1 :, :]
            xs = x_ref[rs, cs].astype(F32) * jnp.exp(end - cum)
            one = dot(bt[:, rs], xs.astype(BF16))
            grown = jnp.exp(end)
            local[b, :, cs] = one
            dec[b : b + 1, cs] = grown
            state = one if state is None else state * grown + one
        tot[:, cs] = state.astype(BF16)
        return carry

    def intra(j, carry):
        cs = lanes_of(j)
        for b in range(blocks):
            rs = slice(b * Q, (b + 1) * Q)
            cum = spread(rs, cs)
            x = x_ref[rs, cs]
            both = []
            for a in range(2):
                gap = cum[:, a * width : a * width + 1] - cumt[pl.ds(2 * j + a, 1), rs]
                grid = jnp.exp(jnp.minimum(gap, 0.0))
                both.append(dot((cross[b] * grid).astype(BF16), x))
            mixed[rs, cs] = (
                jnp.where(lane < width, both[0], both[1]) + skx[0:1, cs] * x.astype(F32)
            )
        return carry

    same = (iota((LANES, LANES), 0) < width) == (iota((LANES, LANES), 1) < width)
    ones = jnp.where(same, 1.0, 0.0).astype(BF16)

    def finish(j, carry):
        cs = lanes_of(j)
        entry = carried[:, cs].astype(F32)
        for b in range(blocks):
            rs = slice(b * Q, (b + 1) * Q)
            c = c_ref[rs, :]
            high = entry.astype(BF16)
            inter = dot(c, high)
            if b:
                inter = inter + dot(c, (entry - high.astype(F32)).astype(BF16))
            value = mixed[rs, cs] + inter * jnp.exp(spread(rs, cs))
            square = value * value
            big = square.astype(BF16)
            small = (square - big.astype(F32)).astype(BF16)
            mean = (dot(big, ones) + dot(small, ones)) * (1.0 / width)
            rec_ref[rs, cs] = (value * lax.rsqrt(mean + 1e-05)).astype(rec_ref.dtype)
            if b + 1 < blocks:
                entry = entry * dec[b : b + 1, cs] + local[b, :, cs]
        return carry

    def off(seen):
        return jnp.where(seen, 0.0, NEG).astype(F32)

    bias = {Z: off(has_z), Y: off(has_y), A: off(has_y), B: off(has_b)}

    def keep(rows, m, l, acc):
        acc_ref[rows, :] = acc
        ml_ref[0, rows, :] = jnp.broadcast_to(m, acc.shape)
        ml_ref[1, rows, :] = jnp.broadcast_to(l, acc.shape)

    def more(h, kind, rows):
        return flash(
            q_ref[rows, lanes_of(h)], [(held[kind, h, 0], held[kind, h, 1], bias[kind], None)],
            ml_ref[0, rows, 0:1], ml_ref[1, rows, 0:1], acc_ref[rows, :],
        )

    query_rows = [slice(r, r + tq) for r in range(0, length, tq)]

    def first_part(h):
        hs = lanes_of(h)
        for rows in query_rows:
            tiles = [(k_ref[rows, hs], v_ref[rows, hs], None, "low")]
            if rows.start > 0:
                tiles.append((k_ref[0 : rows.start, hs], v_ref[0 : rows.start, hs], None, None))
            tiles.append((held[Z, h, 0, rows, :], held[Z, h, 1, rows, :], bias[Z], "up"))
            if rows.stop < length:
                past = slice(rows.stop, length)
                tiles.append((held[Z, h, 0, past, :], held[Z, h, 1, past, :], bias[Z], None))
            tiles.append((held[B, h, 0], held[B, h, 1], bias[B], None))
            keep(rows, *flash(q_ref[rows, hs], tiles, None, None, None))

    def second_part(h):
        for rows in query_rows:
            keep(rows, *more(h, Y, rows))

    def third_part(h):
        for rows in query_rows:
            m, l, acc = more(h, A, rows)
            attn_ref[rows, lanes_of(h)] = (acc / l).astype(attn_ref.dtype)

    @pl.when(z == 0)
    def _():
        def clear(h, carry):
            held[Z, h] = jnp.zeros(held.shape[2:], BF16)

            @pl.when(row == 0)
            def _():
                held[Y, h] = jnp.zeros(held.shape[2:], BF16)
                held[A, h] = jnp.zeros(held.shape[2:], BF16)

            @pl.when(core == 0)
            def _():
                held[B, h] = jnp.zeros(held.shape[2:], BF16)

            return carry

        lax.fori_loop(0, heads, clear, 0)

    def decays(*which):
        for d in which:
            if d:
                own_dl(d).wait_recv()
        line = iota((8, LANES), 0)
        rows = sum(jnp.where(line == i, dl[d], 0.0) for i, d in enumerate(which))
        spread_out = jnp.exp(dot(table(rows[:, :head_count]), hot[...]))
        dtab[which[0] : which[0] + 2, :] = spread_out[0:2, :]

    def chip_totals():
        decays(0, 1)
        for u in range(2):
            to_core(u).wait_recv()
            at = quarter(u, core)
            theirs = jnp.where(core == 1, dtab[0:1, at], 1.0)
            ours = jnp.where(core == 1, 1.0, dtab[1:2, at])
            tc[u] = (theirs * s1[u].astype(F32) + ours * tot[:, at].astype(F32)).astype(BF16)
        to_row().start()

    def pass_state():
        decays(2, 3)
        to_row().wait_recv()

        @pl.when(has_z)
        def _():
            to_next().wait_recv()

        at = quarter(row, core)
        near = dtab[0:1, at] * dtab[1:2, at]
        far = dtab[2:3, at] * dtab[3:4, at]
        entry = ein[...].astype(F32)
        ours, theirs = tc[row].astype(F32), s2[...].astype(F32)
        quad = jnp.where(row == 1, near, 1.0) * theirs + jnp.where(row == 1, 1.0, far) * ours

        @pl.when(has_next)
        def _():
            eout[...] = (near * far * entry + quad).astype(BF16)
            to_next().start()

        s4out[...] = jnp.where(row == 0, near * entry + ours, entry).astype(BF16)
        back_row().start()
        ec[row] = jnp.where(row == 0, entry, far * entry + theirs).astype(BF16)

    def pass_core():
        back_row().wait_recv()
        for u in range(2):
            at = quarter(u, core)
            entry = ec[u].astype(F32)
            later = jnp.where(core == 0, dtab[0:1, at], dtab[1:2, at]) * entry
            later = later + jnp.where(core == 0, tot[:, at], s1[u]).astype(F32)
            s5out[u] = jnp.where(core == 0, later, entry).astype(BF16)
            back_core(u).start()
            carried[:, at] = jnp.where(core == 0, entry, later).astype(BF16)

    turn = jnp.minimum(2 + 2 * z, 8)
    ready = turn + 2
    fourth = pairs // 4

    lax.fori_loop(0, pairs // 2, local_state, 0, unroll=4)
    z_arrived(0, 0, pieces, first_sems)
    lax.fori_loop(pairs // 2, pairs, local_state, 0, unroll=4)
    for u in range(2):
        to_core(u).start()
    for n in range(1, len(pieces)):
        z_arrived(0, n, pieces, first_sems)
    for one in loads[6:]:
        one.wait()

    def step(j, carry):
        @pl.when(j == turn)
        def _():
            pass_state()

        @pl.when((j < heads - 1) & (j >= 1))
        def _():
            for n in range(2):
                z_arrived(j, n, halves, z_sems(j))

        @pl.when(j == heads - 1)
        def _():
            for n in range(len(pieces)):
                z_arrived(heads - 1, n, pieces, last_sems)

        @pl.when(j == 0)
        def _():
            chip_totals()

        @pl.when((j < heads) & has_next)
        def _():
            z_sent(j)

        @pl.when(j + 2 < heads)
        def _():
            @pl.when(j + 3 < heads)
            def _():
                z_offer(j + 2, halves, z_sems(j + 2))

            @pl.when(j + 3 == heads)
            def _():
                z_offer(heads - 1, pieces, last_sems)

            side_offer(j + 2)

        @pl.when(j >= 2)
        def _():
            @pl.when(has_y)
            def _():
                arrived(A, j - 2)

            third_part(j - 2)

        @pl.when((j >= 1) & (j <= heads))
        def _():
            @pl.when(has_b)
            def _():
                arrived(B, j - 1)

            first_part(j - 1)

            @pl.when(has_y)
            def _():
                arrived(Y, j - 1)
                side(A, j - 1, Y).start()

            second_part(j - 1)

        @pl.when(j == turn + 1)
        def _():
            pass_core()

        @pl.when(j < pairs // 2)
        def _():
            for n in range(2):
                intra(2 * j + n, 0)

        @pl.when((j >= ready) & (j < ready + 4))
        def _():
            @pl.when(j == ready)
            def _():
                for u in range(2):
                    back_core(u).wait_recv()

            for n in range(fourth):
                finish((j - ready) * fourth + n, 0)

        return carry

    lax.fori_loop(0, heads + 2, step, 0)

    for d in range(1, 4):
        own_dl(d).wait_send()
    for u in range(2):
        to_core(u).wait_send()
        back_core(u).wait_send()
    to_row().wait_send()
    back_row().wait_send()

    @pl.when(has_next)
    def _():
        to_next().wait_send()

    @pl.when(has_z | (row == 0))
    def _():
        all_sent(Y)

    @pl.when(has_y)
    def _():
        all_sent(A)

    @pl.when(has_z | (core == 0))
    def _():
        all_sent(B)


def on_device(queries, keys, values, ssd_input, bmat, cmat, expo, rate, skip):
    length, total_cols = queries.shape
    size = lax.axis_size("seq")
    head_count = rate.shape[0]
    x_cols = ssd_input.shape[1]
    state = cmat.shape[1]
    heads = total_cols // E
    blocks = length // Q
    group = x_cols // 4
    vmem = pl.BlockSpec(memory_space=pltpu.VMEM)
    dma = pltpu.SemaphoreType.DMA
    inputs = (
        queries, keys, values, ssd_input, bmat, cmat, expo.T, rate[None, :], skip[None, :]
    )
    big = [pltpu.VMEM(a.shape, a.dtype) for a in inputs]
    return pl.pallas_call(
        functools.partial(kernel, size),
        in_specs=[pl.BlockSpec(memory_space=pltpu.HBM)] * len(inputs),
        out_specs=(vmem, vmem),
        out_shape=(
            jax.ShapeDtypeStruct(queries.shape, BF16),
            jax.ShapeDtypeStruct(ssd_input.shape, BF16),
        ),
        scratch_shapes=[
            *big,
            pltpu.VMEM((4, heads, 2, length, E), BF16),
            pltpu.VMEM((LANES, x_cols), BF16),
            pltpu.VMEM((length, LANES), BF16),
            pltpu.VMEM((head_count, length), F32),
            pltpu.VMEM((state, length), BF16),
            pltpu.VMEM((blocks, Q, Q), F32),
            pltpu.VMEM((8, x_cols), F32),
            pltpu.VMEM((8, x_cols), F32),
            pltpu.VMEM((4, 8, LANES), F32),
            pltpu.VMEM((8, x_cols), F32),
            pltpu.VMEM((blocks, state, x_cols), F32),
            pltpu.VMEM((state, x_cols), BF16),
            pltpu.VMEM((2, state, group), BF16),
            pltpu.VMEM((2, state, group), BF16),
            pltpu.VMEM((state, group), BF16),
            pltpu.VMEM((state, group), BF16),
            pltpu.VMEM((state, group), BF16),
            pltpu.VMEM((state, group), BF16),
            pltpu.VMEM((2, state, group), BF16),
            pltpu.VMEM((2, state, group), BF16),
            pltpu.VMEM((state, x_cols), BF16),
            pltpu.VMEM((length, x_cols), F32),
            pltpu.VMEM((length, E), F32),
            pltpu.VMEM((2, length, E), F32),
            dma((9,)),
            dma((heads,)),
            dma((heads, 2)),
            dma((2, 8)),
            dma((3,)),
            dma((3, heads)),
            dma((4,)),
            dma((4,)),
            dma((2,)),
            dma((2,)),
            dma((2,)),
            dma((2,)),
            dma((3,)),
            dma((3,)),
        ],
        compiler_params=pltpu.CompilerParams(
            collective_id=0, has_side_effects=True, vmem_limit_bytes=48 << 20
        ),
        name="attention_and_recurrence",
    )(*(pltpu.with_memory_space_constraint(a, pltpu.HBM) for a in inputs))


def solution(mesh):
    split_rows = P(("groups", "seq"), None)
    return jax.shard_map(
        on_device,
        mesh=mesh,
        in_specs=(split_rows,) * 7 + (P(), P()),
        out_specs=(split_rows, split_rows),
        check_vma=False,
    )
```

```python
import functools
import math

import jax
import jax.numpy as jnp
from jax import lax
from jax.experimental import pallas as pl
from jax.experimental.pallas import tpu as pltpu
from jax.sharding import PartitionSpec as P

E = 128
Q = 256
LANES = 128
NEG = -1e30
LOG2E = math.log2(math.e)
MESH = pl.DeviceIdType.MESH
Z, Y, A, B = range(4)
BF16 = jnp.bfloat16
F32 = jnp.float32


def dot(a, b):
    return jnp.dot(a, b, preferred_element_type=F32)


def dot_t(a, b):
    return lax.dot_general(a, b, (((1,), (1,)), ((), ())), preferred_element_type=F32)


def iota(shape, axis):
    return lax.broadcasted_iota(jnp.int32, shape, axis)


def split(a):
    high = a.astype(BF16)
    rest = a - high.astype(F32)
    middle = rest.astype(BF16)
    return high, middle, (rest - middle.astype(F32)).astype(BF16)


def table(a):
    parts = split(a)
    rest = jnp.zeros((a.shape[0], LANES - 3 * a.shape[1]), BF16)
    return jnp.concatenate([*parts, rest], axis=1)


def wide(a):
    return jnp.concatenate([a, jnp.zeros((a.shape[0], LANES - a.shape[1]), F32)], axis=1)


def lanes_of(j):
    return pl.ds(pl.multiple_of(j * LANES, LANES), LANES)


def flash(q, tiles, m, l, acc):
    tq = q.shape[0]
    scale = LOG2E / math.sqrt(E)
    for k, v, mask in tiles:
        s = dot_t(q, k) * scale
        if mask is not None:
            row, col = iota((tq, tq), 0), iota((tq, tq), 1)
            s = jnp.where(col <= row if mask == "low" else col > row, s, NEG)
        groups = s.shape[1] // LANES
        peak = jnp.broadcast_to(jnp.max(s, axis=1, keepdims=True), (tq, LANES))
        m_new = peak if m is None else jnp.maximum(m, peak)
        p = jnp.exp2(s - jnp.concatenate([m_new] * groups, axis=1))
        total = p[:, 0:LANES]
        for g in range(1, groups):
            total = total + p[:, g * LANES : (g + 1) * LANES]
        part = dot(p.astype(BF16), v)
        if m is None:
            l, acc = total, part
        else:
            alpha = jnp.exp2(m - m_new)
            l = l * alpha + total
            acc = acc * alpha + part
        m = m_new
    return m, l, acc


def whole_sum(l):
    return jnp.sum(l, axis=1, keepdims=True)


def kernel(
    size, q_in, k_in, v_in, x_in, b_in, c_in, expo_in, rate_in, skip_in, attn_ref, rec_ref,
    q_ref, k_ref, v_ref, x_ref, b_ref, c_ref, expo_ref, rate_ref, skip_ref, held, hot, t3, cumt, bt,
    cross, dec, skx, dl, dtab, local, tot, s1, tc, s2, ein, eout, s4out, ec, s5out, carried, mixed,
    acc_ref, ml_ref, q_now, up_q, up_o, up_s, down_o, down_s, row_q, row_o, row_s, back_o, back_s,
    load, z_send, z_recv, last_recv, y_send, y_recv, a_send, a_recv, b_send, b_recv,
    up_q_send, up_q_recv, down_send, down_recv, row_q_send, row_q_recv, back_send, back_recv,
    dl_send, dl_recv, s1_send, s1_recv, s5_send, s5_recv, one_send, one_recv,
):
    nz = size // 4
    here = lax.axis_index("seq")
    mine = lax.axis_index("groups")
    z = here // 4
    member = here % 4
    row = member // 2
    core = member % 2
    length, total_cols = q_ref.shape
    x_cols = x_ref.shape[1]
    heads = total_cols // E
    pairs = x_cols // LANES
    head_count = rate_ref.shape[1]
    width = x_cols // head_count
    group = x_cols // 4
    blocks = length // Q
    tq = min(256, length)
    has_z = z > 0
    has_next = z < nz - 1
    assert heads % nz == 0
    share = heads // nz
    slots = heads - share
    served = share * (nz - 1 - z)
    is_row0 = row == 0
    below = jnp.where(is_row0 | (z == 0), share * (nz - z), share)
    above = jnp.where(is_row0, served, jnp.where(has_next, share, 0))
    swapped = jnp.maximum(above, share)

    def beside(d):
        r = 1 - row if d // 2 else row
        c = 1 - core if d % 2 else core
        return (mine, z * 4 + 2 * r + c)

    def beyond(step):
        return (mine, (z + step + nz) % nz * 4 + member)

    def copy(src, dst, sender, receiver, device):
        return pltpu.make_async_remote_copy(
            src_ref=src, dst_ref=dst, send_sem=sender, recv_sem=receiver,
            device_id=device, device_id_type=MESH,
        )

    inputs = (
        (rate_in, rate_ref), (expo_in, expo_ref), (skip_in, skip_ref), (b_in, b_ref), (c_in, c_ref),
        (x_in, x_ref), (q_in, q_ref), (k_in, k_ref), (v_in, v_ref),
    )
    loads = [pltpu.make_async_copy(a, b, load.at[i]) for i, (a, b) in enumerate(inputs)]
    for one in loads[:6]:
        one.start()

    barrier = pltpu.get_barrier_semaphore()
    for d in range(1, 4):
        pl.semaphore_signal(barrier, inc=1, device_id=beside(d), device_id_type=MESH)

    @pl.when(has_z)
    def _():
        pl.semaphore_signal(barrier, inc=1, device_id=beyond(-1), device_id_type=MESH)

    @pl.when(has_next)
    def _():
        pl.semaphore_signal(barrier, inc=1, device_id=beyond(1), device_id_type=MESH)

    pl.semaphore_wait(barrier, 3 + jnp.minimum(z, 1) + jnp.minimum(nz - 1 - z, 1))

    halves = [(part, slice(0, length)) for part in range(2)]
    piece = length // 4
    pieces = [(part, slice(i * piece, (i + 1) * piece)) for part in range(2) for i in range(4)]

    def y_head(t, to):
        return jnp.where((to == 0) & (t < served), t, share + t)

    def z_copy(t, n, cut):
        part, rows = cut[n]
        h = share + t
        arrival = z_recv.at[t, n] if cut is halves else last_recv.at[n]
        return copy(
            (k_in, v_in)[part].at[rows, lanes_of(h)], held.at[Z, h, part, rows], z_send.at[t],
            arrival, beyond(1),
        )

    def z_arrived(t, cut):
        h = share + t

        @pl.when(has_z & (h >= below))
        def _():
            for n, (part, rows) in enumerate(cut):
                z_copy(t, n, cut).wait_recv()

                @pl.when((row == 1) & (t >= served))
                def _():
                    copy(
                        held.at[Z, h, part, rows], held.at[Y, h, part, rows], y_send.at[t],
                        y_recv.at[t], beside(2),
                    ).start()

                @pl.when(core == 1)
                def _():
                    copy(
                        held.at[Z, h, part, rows], held.at[B, h, part, rows], b_send.at[h],
                        b_recv.at[h], beside(1),
                    ).start()

    def z_sent(t):
        @pl.when(has_next & (share + t >= above))
        def _():
            copy(
                held.at[Z, share + t], held.at[Z, share + t], z_send.at[t], z_recv.at[0, 0], beyond(1)
            ).wait_send()

    def z_offer(t, cut):
        @pl.when(has_next & (share + t >= above))
        def _():
            for n in range(len(cut)):
                z_copy(t, n, cut).start()

    def y_all(t):
        h = y_head(t, row)
        return copy(held.at[Y, h], held.at[Y, h], y_send.at[t], y_recv.at[t], beside(2))

    def a_all(t):
        h = y_head(t, row)
        return copy(held.at[Y, h], held.at[A, h], a_send, a_recv.at[t], beside(1))

    def b_all(h):
        return copy(held.at[B, h], held.at[B, h], b_send.at[h], b_recv.at[h], beside(1))

    def b_own(h):
        for part, ref in ((0, k_in), (1, v_in)):
            copy(
                ref.at[:, lanes_of(h)], held.at[B, h, part], b_send.at[h], b_recv.at[h], beside(1)
            ).start()

    def to_below(h):
        return copy(
            q_in.at[:, lanes_of(h)], up_q.at[h], up_q_send.at[h], up_q_recv.at[h], beyond(-1)
        )

    def to_above(h):
        return (
            copy(down_o.at[h], up_o.at[h], down_send.at[h, 0], down_recv.at[h, 0], beyond(1)),
            copy(down_s.at[h], up_s.at[h], down_send.at[h, 1], down_recv.at[h, 1], beyond(1)),
        )

    def ask_row(h):
        return copy(
            q_in.at[:, lanes_of(h)], row_q.at[h], row_q_send.at[h], row_q_recv.at[h], beside(2)
        )

    def answer_row(h):
        return (
            copy(back_o.at[h], row_o.at[h], back_send.at[h, 0], back_recv.at[h, 0], beside(2)),
            copy(back_s.at[h], row_s.at[h], back_send.at[h, 1], back_recv.at[h, 1], beside(2)),
        )

    def side_offer(t):
        @pl.when((row == 1) & (t < share))
        def _():
            ask_row(t).start()

        @pl.when((row == 0) | (t < served))
        def _():
            h = y_head(t, 1 - row)
            for part, ref in ((0, k_in), (1, v_in)):
                copy(
                    ref.at[:, lanes_of(h)], held.at[Y, h, part], y_send.at[t], y_recv.at[t],
                    beside(2),
                ).start()

        @pl.when(core == 0)
        def _():
            b_own(share + t)

        @pl.when(((core == 0) & (t < share)) | ((core == 1) & (t < swapped)))
        def _():
            b_own(t)

    shift = jnp.where(has_next, above - share, 0)
    z_offer(shift, halves)
    side_offer(0)

    @pl.when(has_z)
    def _():
        def ask(h, carry):
            to_below(h).start()
            return carry

        lax.fori_loop(0, below, ask, 0)

    for one in loads[6:]:
        one.start()

    def own_dl(d):
        return copy(dl.at[0], dl.at[d], dl_send.at[d], dl_recv.at[d], beside(d))

    def quarter(u, c):
        return pl.ds(pl.multiple_of((2 * u + c) * group, group), group)

    def to_core(u):
        return copy(
            tot.at[:, quarter(u, 1 - core)], s1.at[u], s1_send.at[u], s1_recv.at[u], beside(1)
        )

    def to_row():
        return copy(tc.at[1 - row], s2, one_send.at[0], one_recv.at[0], beside(2))

    def to_next():
        return copy(eout, ein, one_send.at[1], one_recv.at[1], beyond(1))

    def back_row():
        return copy(s4out, ec.at[row], one_send.at[2], one_recv.at[2], beside(2))

    def back_core(u):
        return copy(
            s5out.at[u], carried.at[:, quarter(u, core)], s5_send.at[u], s5_recv.at[u], beside(1)
        )

    ki = iota((LANES, x_cols), 0)
    hi = lax.div(iota((LANES, x_cols), 1), width)
    match = ki == hi
    for p in (1, 2):
        match = match | (ki - p * head_count == hi)
    hot[...] = jnp.where(match, 1.0, 0.0).astype(BF16)

    @pl.when(z == 0)
    def _():
        ein[...] = jnp.zeros_like(ein)

    low = iota((Q, Q), 1) <= iota((Q, Q), 0)
    upto = jnp.where(iota((Q, Q), 0) <= iota((Q, Q), 1), 1.0, 0.0).astype(BF16)
    loads[0].wait()
    loads[1].wait()
    rates = wide(rate_ref[...])[0:1, :]
    rates = jnp.broadcast_to(rates, (LANES, LANES)).T[0:head_count, 0:1]
    dlog = None
    for b in range(blocks):
        rs = slice(b * Q, (b + 1) * Q)
        loga = -rates * expo_ref[:, rs].astype(F32)
        sums = sum(dot(part, upto) for part in split(loga))
        cumt[:, rs] = sums
        rest = jnp.zeros((LANES - head_count, Q), F32)
        cum = jnp.concatenate([sums, rest], axis=0).T[:, 0:head_count]
        t3[rs, :] = table(cum)
        last = cum[Q - 1 :, :]
        dlog = last if dlog is None else dlog + last
    dl[0] = jnp.broadcast_to(wide(dlog), dl.shape[1:])
    for d in range(1, 4):
        own_dl(d).start()
    loads[2].wait()
    skx[...] = jnp.broadcast_to(dot(table(skip_ref[...]), hot[...]), skx.shape)
    loads[3].wait()
    loads[4].wait()
    bt[...] = b_ref[...].astype(F32).T.astype(BF16)
    for b in range(blocks):
        rs = slice(b * Q, (b + 1) * Q)
        cross[b] = jnp.where(low, dot_t(c_ref[rs, :], b_ref[rs, :]), 0.0)
    loads[5].wait()

    lane = iota((1, LANES), 1)

    def spread(rs, cs):
        return dot(t3[rs, :], hot[:, cs])

    def local_state(j, carry):
        cs = lanes_of(j)
        state = None
        for b in range(blocks):
            rs = slice(b * Q, (b + 1) * Q)
            cum = spread(rs, cs)
            end = cum[Q - 1 :, :]
            xs = x_ref[rs, cs].astype(F32) * jnp.exp(end - cum)
            one = dot(bt[:, rs], xs.astype(BF16))
            grown = jnp.exp(end)
            local[b, :, cs] = one
            dec[b : b + 1, cs] = grown
            state = one if state is None else state * grown + one
        tot[:, cs] = state.astype(BF16)
        return carry

    def intra(j, carry):
        cs = lanes_of(j)
        for b in range(blocks):
            rs = slice(b * Q, (b + 1) * Q)
            cum = spread(rs, cs)
            x = x_ref[rs, cs]
            both = []
            for a in range(2):
                gap = cum[:, a * width : a * width + 1] - cumt[pl.ds(2 * j + a, 1), rs]
                grid = jnp.exp(jnp.minimum(gap, 0.0))
                both.append(dot((cross[b] * grid).astype(BF16), x))
            mixed[rs, cs] = (
                jnp.where(lane < width, both[0], both[1]) + skx[0:1, cs] * x.astype(F32)
            )
        return carry

    same = (iota((LANES, LANES), 0) < width) == (iota((LANES, LANES), 1) < width)
    ones = jnp.where(same, 1.0, 0.0).astype(BF16)

    def finish(j, carry):
        cs = lanes_of(j)
        entry = carried[:, cs].astype(F32)
        for b in range(blocks):
            rs = slice(b * Q, (b + 1) * Q)
            c = c_ref[rs, :]
            high = entry.astype(BF16)
            inter = dot(c, high)
            if b:
                inter = inter + dot(c, (entry - high.astype(F32)).astype(BF16))
            value = mixed[rs, cs] + inter * jnp.exp(spread(rs, cs))
            square = value * value
            big = square.astype(BF16)
            small = (square - big.astype(F32)).astype(BF16)
            mean = (dot(big, ones) + dot(small, ones)) * (1.0 / width)
            rec_ref[rs, cs] = (value * lax.rsqrt(mean + 1e-05)).astype(rec_ref.dtype)
            if b + 1 < blocks:
                entry = entry * dec[b : b + 1, cs] + local[b, :, cs]
        return carry

    query_rows = [slice(r, r + tq) for r in range(0, length, tq)]

    def keep(slot, rows, m, l, acc):
        acc_ref[slot, rows, :] = acc
        ml_ref[slot, 0, rows, :] = m
        ml_ref[slot, 1, rows, :] = l

    def kept(slot, rows):
        return ml_ref[slot, 0, rows, :], ml_ref[slot, 1, rows, :], acc_ref[slot, rows, :]

    def held_tile(kind, h):
        return (held[kind, h, 0], held[kind, h, 1], None)

    def own_low(h, rows):
        hs = lanes_of(h)
        tiles = [(k_ref[rows, hs], v_ref[rows, hs], "low")]
        if rows.start > 0:
            tiles.append((k_ref[0 : rows.start, hs], v_ref[0 : rows.start, hs], None))
        return tiles

    def own_up(h, rows):
        hs = lanes_of(h)
        tiles = [(k_ref[rows, hs], v_ref[rows, hs], "up")]
        if rows.stop < length:
            tiles.append((k_ref[rows.stop : length, hs], v_ref[rows.stop : length, hs], None))
        return tiles

    def z_up(h, rows):
        tiles = [(held[Z, h, 0, rows, :], held[Z, h, 1, rows, :], "up")]
        if rows.stop < length:
            past = slice(rows.stop, length)
            tiles.append((held[Z, h, 0, past, :], held[Z, h, 1, past, :], None))
        return tiles

    def begin(slot, q_of, tiles_of):
        for rows in query_rows:
            keep(slot, rows, *flash(q_of(rows), tiles_of(rows), None, None, None))

    def emit(m, l, acc, o_ref, s_ref, h, rows):
        l = whole_sum(l)
        o_ref[h, rows, :] = (acc / l).astype(BF16)
        top = m + jnp.log(l) * LOG2E
        s_ref[h, :, rows] = top.T[0:8, :]

    def merge(slot, o_ref, s_ref, h):
        for rows in query_rows:
            m, l, acc = kept(slot, rows)
            top = jnp.concatenate([s_ref[h, :, rows]] * (LANES // 8), axis=0).T
            m_new = jnp.maximum(m, top)
            mine_part, their_part = jnp.exp2(m - m_new), jnp.exp2(top - m_new)
            keep(
                slot, rows, m_new, l * mine_part + jnp.where(lane == 0, their_part, 0.0),
                acc * mine_part + o_ref[h, rows, :].astype(F32) * their_part,
            )

    def finish_head(slot, h):
        for rows in query_rows:
            m, l, acc = kept(slot, rows)
            attn_ref[rows, lanes_of(h)] = (acc / whole_sum(l)).astype(attn_ref.dtype)

    def own_begin(slot, h):
        def q_of(rows):
            return q_ref[rows, lanes_of(h)]

        @pl.when(core == 1)
        def _():
            begin(slot, q_of, lambda rows: own_low(h, rows) + [held_tile(B, h)])

        @pl.when(core == 0)
        def _():
            begin(slot, q_of, lambda rows: own_low(h, rows))

    def serving(t):
        return is_row0 & (t < served)

    def first_part(t):
        @pl.when(serving(t))
        def _():
            to_below(t).wait_recv()
            q_now[...] = up_q[t]

            @pl.when(core == 0)
            def _():
                begin(0, lambda rows: up_q[t, rows, :], lambda rows: own_up(t, rows) + [held_tile(B, t)])

            @pl.when(core == 1)
            def _():
                begin(0, lambda rows: up_q[t, rows, :], lambda rows: own_up(t, rows))

        @pl.when(jnp.logical_not(serving(t)))
        def _():
            h = share + t
            q_now[...] = q_ref[:, lanes_of(h)]

            @pl.when(has_z)
            def _():
                begin(
                    0, lambda rows: q_ref[rows, lanes_of(h)],
                    lambda rows: own_low(h, rows) + z_up(h, rows) + [held_tile(B, h)],
                )

            @pl.when(z == 0)
            def _():
                own_begin(0, h)

    def second_part(t):
        h = y_head(t, row)
        rows = slice(0, length)
        keep(0, rows, *flash(q_now[rows, :], [held_tile(Y, h)], *kept(0, rows)))

    def third_part(t):
        h = y_head(t, row)
        rows = slice(0, length)
        keep(0, rows, *flash(q_now[rows, :], [held_tile(A, h)], *kept(0, rows)))

        @pl.when(serving(t))
        def _():
            for rows in query_rows:
                emit(*kept(0, rows), down_o, down_s, t, rows)
            for one in to_above(t):
                one.start()

        @pl.when(jnp.logical_not(serving(t)))
        def _():
            finish_head(0, h)

    def serve_early(h):
        @pl.when(is_row0)
        def _():
            ask_row(h).wait_recv()
            hs = lanes_of(h)
            for rows in query_rows:
                own = (k_ref[:, hs], v_ref[:, hs], None)
                result = flash(row_q[h, rows, :], [own, held_tile(B, h)], None, None, None)
                emit(*result, back_o, back_s, h, rows)
            for one in answer_row(h):
                one.start()

        @pl.when((row == 1) & has_next)
        def _():
            to_below(h).wait_recv()

            def q_of(rows):
                return up_q[h, rows, :]

            @pl.when(core == 0)
            def _():
                begin(1, q_of, lambda rows: own_up(h, rows) + [held_tile(B, h)])

            @pl.when(core == 1)
            def _():
                begin(1, q_of, lambda rows: own_up(h, rows))

            for rows in query_rows:
                emit(*kept(1, rows), down_o, down_s, h, rows)
            for one in to_above(h):
                one.start()

    def light_head(h, carry):
        own_begin(1, h)

        @pl.when(row == 1)
        def _():
            for one in answer_row(h):
                one.wait_recv()
            merge(1, row_o, row_s, h)

        @pl.when(has_z)
        def _():
            for one in to_above(h):
                one.wait_recv()
            merge(1, up_o, up_s, h)

        finish_head(1, h)
        return carry

    def decays(*which):
        for d in which:
            if d:
                own_dl(d).wait_recv()
        line = iota((8, LANES), 0)
        rows = sum(jnp.where(line == i, dl[d], 0.0) for i, d in enumerate(which))
        spread_out = jnp.exp(dot(table(rows[:, :head_count]), hot[...]))
        dtab[which[0] : which[0] + 2, :] = spread_out[0:2, :]

    def chip_totals():
        decays(0, 1)
        for u in range(2):
            to_core(u).wait_recv()
            at = quarter(u, core)
            theirs = jnp.where(core == 1, dtab[0:1, at], 1.0)
            ours = jnp.where(core == 1, 1.0, dtab[1:2, at])
            tc[u] = (theirs * s1[u].astype(F32) + ours * tot[:, at].astype(F32)).astype(BF16)
        to_row().start()

    def pass_state():
        decays(2, 3)
        to_row().wait_recv()

        @pl.when(has_z)
        def _():
            to_next().wait_recv()

        at = quarter(row, core)
        near = dtab[0:1, at] * dtab[1:2, at]
        far = dtab[2:3, at] * dtab[3:4, at]
        entry = ein[...].astype(F32)
        ours, theirs = tc[row].astype(F32), s2[...].astype(F32)
        quad = jnp.where(row == 1, near, 1.0) * theirs + jnp.where(row == 1, 1.0, far) * ours

        @pl.when(has_next)
        def _():
            eout[...] = (near * far * entry + quad).astype(BF16)
            to_next().start()

        @pl.when(has_z | is_row0)
        def _():
            s4out[...] = jnp.where(row == 0, near * entry + ours, entry).astype(BF16)
            back_row().start()

        @pl.when((z == 0) & is_row0)
        def _():
            ec[1] = jnp.zeros(ec.shape[1:], BF16)

        ec[row] = jnp.where(row == 0, entry, far * entry + theirs).astype(BF16)

    def pass_core():
        @pl.when(has_z | (row == 1))
        def _():
            back_row().wait_recv()

        for u in range(2):
            at = quarter(u, core)
            entry = ec[u].astype(F32)
            later = jnp.where(core == 0, dtab[0:1, at], dtab[1:2, at]) * entry
            later = later + jnp.where(core == 0, tot[:, at], s1[u]).astype(F32)
            s5out[u] = jnp.where(core == 0, later, entry).astype(BF16)
            back_core(u).start()
            carried[:, at] = jnp.where(core == 0, entry, later).astype(BF16)

    turn = jnp.minimum(2 + (3 * z + 1) // 2, 7)
    back = jnp.where(z < 2, turn + 2, turn + 1)
    ready = back + 1
    units = pairs // 2
    lights = jnp.where(row == 1, share, below)

    free = is_row0 & (z == 0)

    def light_range(j):
        count = jnp.where(j <= share, 2, 1)
        count = jnp.where((j >= 1) & (j <= slots), count, 0)
        first = jnp.clip(j - 3, 0, lights)
        last = jnp.clip(j - 2, 0, lights)
        return jnp.where(free, 0, first), jnp.where(free, count, last)

    lax.fori_loop(0, pairs, local_state, 0, unroll=4)
    for u in range(2):
        to_core(u).start()
    for one in loads[6:]:
        one.wait()

    def step(j, carry):
        @pl.when(j == turn)
        def _():
            pass_state()

        @pl.when(j < slots - 1)
        def _():
            z_arrived(j, halves)

        @pl.when(j == slots - 1)
        def _():
            z_arrived(slots - 1, pieces)

        @pl.when(j == 0)
        def _():
            chip_totals()
            z_offer(1 + shift, halves)
            side_offer(1)

        @pl.when((j >= 1) & (j <= slots))
        def _():
            @pl.when(j - 1 + shift < slots)
            def _():
                z_sent(j - 1 + shift)

            @pl.when((row == 0) | (j - 1 < served))
            def _():
                y_all(j - 1).wait_send()

        @pl.when(j + 3 + shift < slots)
        def _():
            z_offer(j + 2 + shift, halves)

        @pl.when(j + 3 + shift == slots)
        def _():
            z_offer(slots - 1, pieces)

        @pl.when(j + 2 < slots)
        def _():
            side_offer(j + 2)

        @pl.when((j >= 2) & (j < slots + 2))
        def _():
            a_all(j - 2).wait_recv()
            third_part(j - 2)

        @pl.when((j >= 1) & (j <= slots))
        def _():
            t = j - 1

            @pl.when((t < share) | ((core == 0) & (t < swapped)))
            def _():
                b_all(t).wait_recv()

            @pl.when((core == 1) | (has_z & (share + t >= below)))
            def _():
                b_all(share + t).wait_recv()

            @pl.when(t < share)
            def _():
                serve_early(t)

            first_part(t)
            y_all(t).wait_recv()
            a_all(t).start()
            second_part(t)

        def light(i, carry):
            waiting = jnp.where(i == 0, share + j - 1, j - 1)
            return light_head(jnp.where(free, waiting, i), carry)

        lax.fori_loop(*light_range(j), light, 0)

        @pl.when(j == back)
        def _():
            pass_core()

        @pl.when(j < 4)
        def _():
            for n in range(pairs // 4):
                intra(pairs // 4 * j + n, 0)

        @pl.when(j == ready)
        def _():
            for u in range(2):
                back_core(u).wait_recv()

        def finish_two(n, carry):
            finish(2 * n, carry)
            return finish(2 * n + 1, carry)

        first = jnp.clip(3 * (j - ready), 0, units)
        lax.fori_loop(first, jnp.clip(3 * (j - ready + 1), 0, units), finish_two, 0)

        return carry

    lax.fori_loop(0, slots + 3, step, 0)

    for d in range(1, 4):
        own_dl(d).wait_send()
    for u in range(2):
        to_core(u).wait_send()
        back_core(u).wait_send()
    to_row().wait_send()

    @pl.when(has_z | is_row0)
    def _():
        back_row().wait_send()

    @pl.when(has_next)
    def _():
        to_next().wait_send()

    copy(
        held.at[Y, pl.ds(0, slots)], held.at[A, pl.ds(0, slots)], a_send, a_recv.at[0], beside(1)
    ).wait_send()

    def drain(h, carry):
        @pl.when((core == 0) | (h < swapped) | (has_z & (h >= below)))
        def _():
            b_all(h).wait_send()

        @pl.when(has_z & (h < below))
        def _():
            to_below(h).wait_send()

        @pl.when(has_next & (h < above))
        def _():
            for one in to_above(h):
                one.wait_send()

        @pl.when((h < slots) & (row == 1) & (h >= served))
        def _():
            y_all(h).wait_send()

        @pl.when((h < share) & (row == 1))
        def _():
            ask_row(h).wait_send()

        @pl.when((h < share) & (row == 0))
        def _():
            for one in answer_row(h):
                one.wait_send()

        return carry

    lax.fori_loop(0, heads, drain, 0)


def on_device(queries, keys, values, ssd_input, bmat, cmat, expo, rate, skip):
    length, total_cols = queries.shape
    size = lax.axis_size("seq")
    head_count = rate.shape[0]
    x_cols = ssd_input.shape[1]
    state = cmat.shape[1]
    heads = total_cols // E
    blocks = length // Q
    group = x_cols // 4
    share = heads // (size // 4)
    slots = heads - share
    vmem = pl.BlockSpec(memory_space=pltpu.VMEM)
    dma = pltpu.SemaphoreType.DMA
    inputs = (
        queries, keys, values, ssd_input, bmat, cmat, expo.T, rate[None, :], skip[None, :]
    )
    big = [pltpu.VMEM(a.shape, a.dtype) for a in inputs]
    return pl.pallas_call(
        functools.partial(kernel, size),
        in_specs=[pl.BlockSpec(memory_space=pltpu.HBM)] * len(inputs),
        out_specs=(vmem, vmem),
        out_shape=(
            jax.ShapeDtypeStruct(queries.shape, BF16),
            jax.ShapeDtypeStruct(ssd_input.shape, BF16),
        ),
        scratch_shapes=[
            *big,
            pltpu.VMEM((4, heads, 2, length, E), BF16),
            pltpu.VMEM((LANES, x_cols), BF16),
            pltpu.VMEM((length, LANES), BF16),
            pltpu.VMEM((head_count, length), F32),
            pltpu.VMEM((state, length), BF16),
            pltpu.VMEM((blocks, Q, Q), F32),
            pltpu.VMEM((8, x_cols), F32),
            pltpu.VMEM((8, x_cols), F32),
            pltpu.VMEM((4, 8, LANES), F32),
            pltpu.VMEM((8, x_cols), F32),
            pltpu.VMEM((blocks, state, x_cols), F32),
            pltpu.VMEM((state, x_cols), BF16),
            pltpu.VMEM((2, state, group), BF16),
            pltpu.VMEM((2, state, group), BF16),
            pltpu.VMEM((state, group), BF16),
            pltpu.VMEM((state, group), BF16),
            pltpu.VMEM((state, group), BF16),
            pltpu.VMEM((state, group), BF16),
            pltpu.VMEM((2, state, group), BF16),
            pltpu.VMEM((2, state, group), BF16),
            pltpu.VMEM((state, x_cols), BF16),
            pltpu.VMEM((length, x_cols), F32),
            pltpu.VMEM((2, length, E), F32),
            pltpu.VMEM((2, 2, length, E), F32),
            pltpu.VMEM((length, E), BF16),
            pltpu.VMEM((heads, length, E), BF16),
            pltpu.VMEM((heads, length, E), BF16),
            pltpu.VMEM((heads, 8, length), F32),
            pltpu.VMEM((heads, length, E), BF16),
            pltpu.VMEM((heads, 8, length), F32),
            pltpu.VMEM((share, length, E), BF16),
            pltpu.VMEM((share, length, E), BF16),
            pltpu.VMEM((share, 8, length), F32),
            pltpu.VMEM((share, length, E), BF16),
            pltpu.VMEM((share, 8, length), F32),
            dma((9,)),
            dma((slots,)),
            dma((slots, 2)),
            dma((8,)),
            dma((slots,)),
            dma((slots,)),
            dma,
            dma((slots,)),
            dma((heads,)),
            dma((heads,)),
            dma((heads,)),
            dma((heads,)),
            dma((heads, 2)),
            dma((heads, 2)),
            dma((share,)),
            dma((share,)),
            dma((share, 2)),
            dma((share, 2)),
            dma((4,)),
            dma((4,)),
            dma((2,)),
            dma((2,)),
            dma((2,)),
            dma((2,)),
            dma((3,)),
            dma((3,)),
        ],
        compiler_params=pltpu.CompilerParams(
            collective_id=0, has_side_effects=True, vmem_limit_bytes=48 << 20
        ),
        name="attention_and_recurrence",
    )(*(pltpu.with_memory_space_constraint(a, pltpu.HBM) for a in inputs))


def solution(mesh):
    split_rows = P(("groups", "seq"), None)
    return jax.shard_map(
        on_device,
        mesh=mesh,
        in_specs=(split_rows,) * 7 + (P(), P()),
        out_specs=(split_rows, split_rows),
        check_vma=False,
    )
```

```python
import functools
import math

import jax
import jax.numpy as jnp
from jax import lax
from jax.experimental import pallas as pl
from jax.experimental.pallas import tpu as pltpu
from jax.sharding import PartitionSpec as P

E = 128
Q = 256
LANES = 128
NEG = -1e30
LOG2E = math.log2(math.e)
MESH = pl.DeviceIdType.MESH
Z, Y, A, B = range(4)
BF16 = jnp.bfloat16
F32 = jnp.float32


def dot(a, b):
    return jnp.dot(a, b, preferred_element_type=F32)


def dot_t(a, b):
    return lax.dot_general(a, b, (((1,), (1,)), ((), ())), preferred_element_type=F32)


def iota(shape, axis):
    return lax.broadcasted_iota(jnp.int32, shape, axis)


def split(a):
    high = a.astype(BF16)
    rest = a - high.astype(F32)
    middle = rest.astype(BF16)
    return high, middle, (rest - middle.astype(F32)).astype(BF16)


def table(a):
    parts = split(a)
    rest = jnp.zeros((a.shape[0], LANES - 3 * a.shape[1]), BF16)
    return jnp.concatenate([*parts, rest], axis=1)


def wide(a):
    return jnp.concatenate([a, jnp.zeros((a.shape[0], LANES - a.shape[1]), F32)], axis=1)


def lanes_of(j):
    return pl.ds(pl.multiple_of(j * LANES, LANES), LANES)


def flash(q, tiles, m, l, acc):
    tq = q.shape[0]
    scale = LOG2E / math.sqrt(E)
    for k, v, mask in tiles:
        s = dot_t(q, k) * scale
        if mask is not None:
            row, col = iota((tq, tq), 0), iota((tq, tq), 1)
            s = jnp.where(col <= row if mask == "low" else col > row, s, NEG)
        groups = s.shape[1] // LANES
        peak = jnp.broadcast_to(jnp.max(s, axis=1, keepdims=True), (tq, LANES))
        m_new = peak if m is None else jnp.maximum(m, peak)
        p = jnp.exp2(s - jnp.concatenate([m_new] * groups, axis=1))
        total = p[:, 0:LANES]
        for g in range(1, groups):
            total = total + p[:, g * LANES : (g + 1) * LANES]
        part = dot(p.astype(BF16), v)
        if m is None:
            l, acc = total, part
        else:
            alpha = jnp.exp2(m - m_new)
            l = l * alpha + total
            acc = acc * alpha + part
        m = m_new
    return m, l, acc


def whole_sum(l):
    return jnp.sum(l, axis=1, keepdims=True)


def kernel(
    size, q_in, k_in, v_in, x_in, b_in, c_in, expo_in, rate_in, skip_in, attn_ref, rec_ref,
    q_ref, k_ref, v_ref, x_ref, b_ref, c_ref, expo_ref, rate_ref, skip_ref, held, hot, t3, cumt, bt,
    cross, dec, skx, dl, dtab, local, tot, s1, tc, s2, ein, eout, s4out, ec, s5out, carried, mixed,
    acc_ref, ml_ref, q_now, up_q, up_o, up_s, down_o, down_s, row_q, row_o, row_s, back_o, back_s,
    load, z_send, z_recv, last_recv, y_send, y_recv, a_send, a_recv, b_send, b_recv,
    y_relay_send, up_q_send, up_q_recv, down_send, down_recv, row_q_send, row_q_recv, back_send, back_recv,
    dl_send, dl_recv, s1_send, s1_recv, s5_send, s5_recv, one_send, one_recv,
):
    nz = size // 4
    here = lax.axis_index("seq")
    mine = lax.axis_index("groups")
    z = here // 4
    member = here % 4
    row = member // 2
    core = member % 2
    length, total_cols = q_ref.shape
    x_cols = x_ref.shape[1]
    heads = total_cols // E
    pairs = x_cols // LANES
    head_count = rate_ref.shape[1]
    width = x_cols // head_count
    group = x_cols // 4
    blocks = length // Q
    tq = min(256, length)
    has_z = z > 0
    has_next = z < nz - 1
    assert heads % nz == 0
    share = heads // nz
    slots = heads - share
    served = share * (nz - 1 - z)
    is_row0 = row == 0
    below = jnp.where(is_row0 | (z == 0), share * (nz - z), share)
    above = jnp.where(is_row0, served, jnp.where(has_next, share, 0))
    swapped = jnp.maximum(above, share)

    def beside(d):
        r = 1 - row if d // 2 else row
        c = 1 - core if d % 2 else core
        return (mine, z * 4 + 2 * r + c)

    def beyond(step):
        return (mine, (z + step + nz) % nz * 4 + member)

    def copy(src, dst, sender, receiver, device):
        return pltpu.make_async_remote_copy(
            src_ref=src, dst_ref=dst, send_sem=sender, recv_sem=receiver,
            device_id=device, device_id_type=MESH,
        )

    inputs = (
        (rate_in, rate_ref), (expo_in, expo_ref), (skip_in, skip_ref), (b_in, b_ref), (c_in, c_ref),
        (x_in, x_ref), (q_in, q_ref), (k_in, k_ref), (v_in, v_ref),
    )
    loads = [pltpu.make_async_copy(a, b, load.at[i]) for i, (a, b) in enumerate(inputs)]
    for one in loads[:6]:
        one.start()

    barrier = pltpu.get_barrier_semaphore()
    for d in range(1, 4):
        pl.semaphore_signal(barrier, inc=1, device_id=beside(d), device_id_type=MESH)

    @pl.when(has_z)
    def _():
        pl.semaphore_signal(barrier, inc=1, device_id=beyond(-1), device_id_type=MESH)

    @pl.when(has_next)
    def _():
        pl.semaphore_signal(barrier, inc=1, device_id=beyond(1), device_id_type=MESH)

    pl.semaphore_wait(barrier, 3 + jnp.minimum(z, 1) + jnp.minimum(nz - 1 - z, 1))

    def team(h):
        return lax.div(h, share)

    halves = [(part, slice(0, length)) for part in range(2)]
    piece = length // 4
    pieces = [(part, slice(i * piece, (i + 1) * piece)) for part in range(2) for i in range(4)]

    def y_head(t, to):
        return jnp.where((to == 0) & (t < served), t, share + t)

    def z_copy(t, n, cut):
        part, rows = cut[n]
        h = share + t
        arrival = z_recv.at[t, n] if cut is halves else last_recv.at[n]
        return copy(
            (k_in, v_in)[part].at[rows, lanes_of(h)], held.at[Z, h, part, rows], z_send.at[t],
            arrival, beyond(1),
        )

    def z_arrived(t, cut):
        h = share + t

        @pl.when(has_z & (h >= below))
        def _():
            for n, (part, rows) in enumerate(cut):
                z_copy(t, n, cut).wait_recv()

                @pl.when((row == 1) & (t >= served))
                def _():
                    copy(
                        held.at[Z, h, part, rows], held.at[Y, h, part, rows],
                        y_relay_send.at[team(t)], y_recv.at[t], beside(2),
                    ).start()

                @pl.when(core == 1)
                def _():
                    copy(
                        held.at[Z, h, part, rows], held.at[B, h, part, rows], b_send.at[team(h)],
                        b_recv.at[h], beside(1),
                    ).start()

    def z_sent(t):
        @pl.when(has_next & (share + t >= above))
        def _():
            copy(
                held.at[Z, share + t], held.at[Z, share + t], z_send.at[t], z_recv.at[0, 0], beyond(1)
            ).wait_send()

    def z_offer(t, cut):
        @pl.when(has_next & (share + t >= above))
        def _():
            for n in range(len(cut)):
                z_copy(t, n, cut).start()

    def y_all(t):
        h = y_head(t, row)
        return copy(held.at[Y, h], held.at[Y, h], y_send.at[t], y_recv.at[t], beside(2))

    def a_all(t):
        h = y_head(t, row)
        return copy(held.at[Y, h], held.at[A, h], a_send, a_recv.at[t], beside(1))

    def b_all(h):
        return copy(held.at[B, h], held.at[B, h], b_send.at[0], b_recv.at[h], beside(1))

    def b_own(h):
        for part, ref in ((0, k_in), (1, v_in)):
            copy(
                ref.at[:, lanes_of(h)], held.at[B, h, part], b_send.at[team(h)], b_recv.at[h],
                beside(1),
            ).start()

    def to_below(h):
        return copy(
            q_in.at[:, lanes_of(h)], up_q.at[h], up_q_send.at[team(h)], up_q_recv.at[h], beyond(-1)
        )

    def to_above(h):
        return (
            copy(down_o.at[h], up_o.at[h], down_send.at[team(h), 0], down_recv.at[h, 0], beyond(1)),
            copy(down_s.at[h], up_s.at[h], down_send.at[team(h), 1], down_recv.at[h, 1], beyond(1)),
        )

    def ask_row(h):
        return copy(
            q_in.at[:, lanes_of(h)], row_q.at[h], row_q_send, row_q_recv.at[h], beside(2)
        )

    def answer_row(h):
        return (
            copy(back_o.at[h], row_o.at[h], back_send.at[0], back_recv.at[h, 0], beside(2)),
            copy(back_s.at[h], row_s.at[h], back_send.at[1], back_recv.at[h, 1], beside(2)),
        )

    def side_offer(t):
        @pl.when((row == 1) & (t < share))
        def _():
            ask_row(t).start()

        @pl.when((row == 0) | (t < served))
        def _():
            h = y_head(t, 1 - row)
            for part, ref in ((0, k_in), (1, v_in)):
                copy(
                    ref.at[:, lanes_of(h)], held.at[Y, h, part], y_send.at[t], y_recv.at[t],
                    beside(2),
                ).start()

        @pl.when(core == 0)
        def _():
            b_own(share + t)

        @pl.when(((core == 0) & (t < share)) | ((core == 1) & (t < swapped)))
        def _():
            b_own(t)

    shift = jnp.where(has_next, above - share, 0)
    z_offer(shift, halves)
    side_offer(0)

    @pl.when(has_z)
    def _():
        def ask(h, carry):
            to_below(h).start()
            return carry

        lax.fori_loop(0, below, ask, 0)

    for one in loads[6:]:
        one.start()

    def own_dl(d):
        return copy(dl.at[0], dl.at[d], dl_send.at[d], dl_recv.at[d], beside(d))

    def quarter(u, c):
        return pl.ds(pl.multiple_of((2 * u + c) * group, group), group)

    def to_core(u):
        return copy(
            tot.at[:, quarter(u, 1 - core)], s1.at[u], s1_send.at[u], s1_recv.at[u], beside(1)
        )

    def to_row():
        return copy(tc.at[1 - row], s2, one_send.at[0], one_recv.at[0], beside(2))

    def to_next():
        return copy(eout, ein, one_send.at[1], one_recv.at[1], beyond(1))

    def back_row():
        return copy(s4out, ec.at[row], one_send.at[2], one_recv.at[2], beside(2))

    def back_core(u):
        return copy(
            s5out.at[u], carried.at[:, quarter(u, core)], s5_send.at[u], s5_recv.at[u], beside(1)
        )

    ki = iota((LANES, x_cols), 0)
    hi = lax.div(iota((LANES, x_cols), 1), width)
    match = ki == hi
    for p in (1, 2):
        match = match | (ki - p * head_count == hi)
    hot[...] = jnp.where(match, 1.0, 0.0).astype(BF16)

    @pl.when(z == 0)
    def _():
        ein[...] = jnp.zeros_like(ein)

    low = iota((Q, Q), 1) <= iota((Q, Q), 0)
    upto = jnp.where(iota((Q, Q), 0) <= iota((Q, Q), 1), 1.0, 0.0).astype(BF16)
    loads[0].wait()
    loads[1].wait()
    rates = wide(rate_ref[...])[0:1, :]
    rates = jnp.broadcast_to(rates, (LANES, LANES)).T[0:head_count, 0:1]
    dlog = None
    for b in range(blocks):
        rs = slice(b * Q, (b + 1) * Q)
        loga = -rates * expo_ref[:, rs].astype(F32)
        sums = sum(dot(part, upto) for part in split(loga))
        cumt[:, rs] = sums
        rest = jnp.zeros((LANES - head_count, Q), F32)
        cum = jnp.concatenate([sums, rest], axis=0).T[:, 0:head_count]
        t3[rs, :] = table(cum)
        last = cum[Q - 1 :, :]
        dlog = last if dlog is None else dlog + last
    dl[0] = jnp.broadcast_to(wide(dlog), dl.shape[1:])
    for d in range(1, 4):
        own_dl(d).start()
    loads[2].wait()
    skx[...] = jnp.broadcast_to(dot(table(skip_ref[...]), hot[...]), skx.shape)
    loads[3].wait()
    loads[4].wait()
    bt[...] = b_ref[...].astype(F32).T.astype(BF16)
    for b in range(blocks):
        rs = slice(b * Q, (b + 1) * Q)
        cross[b] = jnp.where(low, dot_t(c_ref[rs, :], b_ref[rs, :]), 0.0)
    loads[5].wait()

    lane = iota((1, LANES), 1)

    def spread(rs, cs):
        return dot(t3[rs, :], hot[:, cs])

    def local_state(j, carry):
        cs = lanes_of(j)
        state = None
        for b in range(blocks):
            rs = slice(b * Q, (b + 1) * Q)
            cum = spread(rs, cs)
            end = cum[Q - 1 :, :]
            xs = x_ref[rs, cs].astype(F32) * jnp.exp(end - cum)
            one = dot(bt[:, rs], xs.astype(BF16))
            grown = jnp.exp(end)
            local[b, :, cs] = one
            dec[b : b + 1, cs] = grown
            state = one if state is None else state * grown + one
        tot[:, cs] = state.astype(BF16)
        return carry

    def intra(j, carry):
        cs = lanes_of(j)
        for b in range(blocks):
            rs = slice(b * Q, (b + 1) * Q)
            cum = spread(rs, cs)
            x = x_ref[rs, cs]
            both = []
            for a in range(2):
                gap = cum[:, a * width : a * width + 1] - cumt[pl.ds(2 * j + a, 1), rs]
                grid = jnp.exp(jnp.minimum(gap, 0.0))
                both.append(dot((cross[b] * grid).astype(BF16), x))
            mixed[rs, cs] = (
                jnp.where(lane < width, both[0], both[1]) + skx[0:1, cs] * x.astype(F32)
            )
        return carry

    same = (iota((LANES, LANES), 0) < width) == (iota((LANES, LANES), 1) < width)
    ones = jnp.where(same, 1.0, 0.0).astype(BF16)

    def finish(j, carry):
        cs = lanes_of(j)
        entry = carried[:, cs].astype(F32)
        for b in range(blocks):
            rs = slice(b * Q, (b + 1) * Q)
            c = c_ref[rs, :]
            high = entry.astype(BF16)
            inter = dot(c, high)
            if b:
                inter = inter + dot(c, (entry - high.astype(F32)).astype(BF16))
            value = mixed[rs, cs] + inter * jnp.exp(spread(rs, cs))
            square = value * value
            big = square.astype(BF16)
            small = (square - big.astype(F32)).astype(BF16)
            mean = (dot(big, ones) + dot(small, ones)) * (1.0 / width)
            rec_ref[rs, cs] = (value * lax.rsqrt(mean + 1e-05)).astype(rec_ref.dtype)
            if b + 1 < blocks:
                entry = entry * dec[b : b + 1, cs] + local[b, :, cs]
        return carry

    query_rows = [slice(r, r + tq) for r in range(0, length, tq)]

    def keep(slot, rows, m, l, acc):
        acc_ref[slot, rows, :] = acc
        ml_ref[slot, 0, rows, :] = m
        ml_ref[slot, 1, rows, :] = l

    def kept(slot, rows):
        return ml_ref[slot, 0, rows, :], ml_ref[slot, 1, rows, :], acc_ref[slot, rows, :]

    def held_tile(kind, h):
        return (held[kind, h, 0], held[kind, h, 1], None)

    def own_low(h, rows):
        hs = lanes_of(h)
        tiles = [(k_ref[rows, hs], v_ref[rows, hs], "low")]
        if rows.start > 0:
            tiles.append((k_ref[0 : rows.start, hs], v_ref[0 : rows.start, hs], None))
        return tiles

    def own_up(h, rows):
        hs = lanes_of(h)
        tiles = [(k_ref[rows, hs], v_ref[rows, hs], "up")]
        if rows.stop < length:
            tiles.append((k_ref[rows.stop : length, hs], v_ref[rows.stop : length, hs], None))
        return tiles

    def z_up(h, rows):
        tiles = [(held[Z, h, 0, rows, :], held[Z, h, 1, rows, :], "up")]
        if rows.stop < length:
            past = slice(rows.stop, length)
            tiles.append((held[Z, h, 0, past, :], held[Z, h, 1, past, :], None))
        return tiles

    def begin(slot, q_of, tiles_of):
        for rows in query_rows:
            keep(slot, rows, *flash(q_of(rows), tiles_of(rows), None, None, None))

    def emit(m, l, acc, o_ref, s_ref, h, rows):
        l = whole_sum(l)
        o_ref[h, rows, :] = (acc / l).astype(BF16)
        top = m + jnp.log(l) * LOG2E
        s_ref[h, :, rows] = top.T[0:8, :]

    def merge(slot, o_ref, s_ref, h):
        for rows in [slice(0, length)]:
            m, l, acc = kept(slot, rows)
            top = jnp.concatenate([s_ref[h, :, rows]] * (LANES // 8), axis=0).T
            m_new = jnp.maximum(m, top)
            mine_part, their_part = jnp.exp2(m - m_new), jnp.exp2(top - m_new)
            keep(
                slot, rows, m_new, l * mine_part + jnp.where(lane == 0, their_part, 0.0),
                acc * mine_part + o_ref[h, rows, :].astype(F32) * their_part,
            )

    def finish_head(slot, h):
        for rows in [slice(0, length)]:
            m, l, acc = kept(slot, rows)
            attn_ref[rows, lanes_of(h)] = (acc / whole_sum(l)).astype(attn_ref.dtype)

    def extend(slot, q, tile):
        rows = slice(0, length)
        keep(slot, rows, *flash(q, [tile], *kept(slot, rows)))

    def own_begin(slot, h):
        hs = lanes_of(h)
        begin(slot, lambda rows: q_ref[rows, hs], lambda rows: own_low(h, rows))

        @pl.when(core == 1)
        def _():
            extend(slot, q_ref[:, hs], held_tile(B, h))

    def serving(t):
        return is_row0 & (t < served)

    def first_part(t):
        @pl.when(serving(t))
        def _():
            to_below(t).wait_recv()
            q_now[...] = up_q[t]

            begin(0, lambda rows: up_q[t, rows, :], lambda rows: own_up(t, rows))

            @pl.when(core == 0)
            def _():
                extend(0, up_q[t], held_tile(B, t))

        @pl.when(jnp.logical_not(serving(t)))
        def _():
            h = share + t
            q_now[...] = q_ref[:, lanes_of(h)]

            @pl.when(has_z)
            def _():
                begin(
                    0, lambda rows: q_ref[rows, lanes_of(h)],
                    lambda rows: own_low(h, rows) + z_up(h, rows),
                )
                extend(0, q_ref[:, lanes_of(h)], held_tile(B, h))

            @pl.when(z == 0)
            def _():
                own_begin(0, h)

    def second_part(t):
        h = y_head(t, row)
        rows = slice(0, length)
        keep(0, rows, *flash(q_now[rows, :], [held_tile(Y, h)], *kept(0, rows)))

    def third_part(t):
        h = y_head(t, row)
        rows = slice(0, length)
        keep(0, rows, *flash(q_now[rows, :], [held_tile(A, h)], *kept(0, rows)))

        @pl.when(serving(t))
        def _():
            for rows in [slice(0, length)]:
                emit(*kept(0, rows), down_o, down_s, t, rows)
            for one in to_above(t):
                one.start()

        @pl.when(jnp.logical_not(serving(t)))
        def _():
            finish_head(0, h)

    def serve_early(h):
        @pl.when(is_row0)
        def _():
            ask_row(h).wait_recv()
            hs = lanes_of(h)
            own = (k_ref[:, hs], v_ref[:, hs], None)
            result = flash(row_q[h], [own, held_tile(B, h)], None, None, None)
            emit(*result, back_o, back_s, h, slice(0, length))
            for one in answer_row(h):
                one.start()

        @pl.when((row == 1) & has_next)
        def _():
            to_below(h).wait_recv()

            begin(1, lambda rows: up_q[h, rows, :], lambda rows: own_up(h, rows))

            @pl.when(core == 0)
            def _():
                extend(1, up_q[h], held_tile(B, h))

            for rows in [slice(0, length)]:
                emit(*kept(1, rows), down_o, down_s, h, rows)
            for one in to_above(h):
                one.start()

    def light_head(h, carry):
        own_begin(1, h)

        @pl.when(row == 1)
        def _():
            for one in answer_row(h):
                one.wait_recv()
            merge(1, row_o, row_s, h)

        @pl.when(has_z)
        def _():
            for one in to_above(h):
                one.wait_recv()
            merge(1, up_o, up_s, h)

        finish_head(1, h)
        return carry

    def decays(*which):
        for d in which:
            if d:
                own_dl(d).wait_recv()
        line = iota((8, LANES), 0)
        rows = sum(jnp.where(line == i, dl[d], 0.0) for i, d in enumerate(which))
        spread_out = jnp.exp(dot(table(rows[:, :head_count]), hot[...]))
        dtab[which[0] : which[0] + 2, :] = spread_out[0:2, :]

    def chip_totals():
        decays(0, 1)
        for u in range(2):
            to_core(u).wait_recv()
            at = quarter(u, core)
            theirs = jnp.where(core == 1, dtab[0:1, at], 1.0)
            ours = jnp.where(core == 1, 1.0, dtab[1:2, at])
            tc[u] = (theirs * s1[u].astype(F32) + ours * tot[:, at].astype(F32)).astype(BF16)
        to_row().start()

    def pass_state():
        decays(2, 3)
        to_row().wait_recv()

        @pl.when(has_z)
        def _():
            to_next().wait_recv()

        at = quarter(row, core)
        near = dtab[0:1, at] * dtab[1:2, at]
        far = dtab[2:3, at] * dtab[3:4, at]
        entry = ein[...].astype(F32)
        ours, theirs = tc[row].astype(F32), s2[...].astype(F32)
        quad = jnp.where(row == 1, near, 1.0) * theirs + jnp.where(row == 1, 1.0, far) * ours

        @pl.when(has_next)
        def _():
            eout[...] = (near * far * entry + quad).astype(BF16)
            to_next().start()

        @pl.when(has_z | is_row0)
        def _():
            s4out[...] = jnp.where(row == 0, near * entry + ours, entry).astype(BF16)
            back_row().start()

        @pl.when((z == 0) & is_row0)
        def _():
            ec[1] = jnp.zeros(ec.shape[1:], BF16)

        ec[row] = jnp.where(row == 0, entry, far * entry + theirs).astype(BF16)

    def pass_core():
        @pl.when(has_z | (row == 1))
        def _():
            back_row().wait_recv()

        for u in range(2):
            at = quarter(u, core)
            entry = ec[u].astype(F32)
            later = jnp.where(core == 0, dtab[0:1, at], dtab[1:2, at]) * entry
            later = later + jnp.where(core == 0, tot[:, at], s1[u]).astype(F32)
            s5out[u] = jnp.where(core == 0, later, entry).astype(BF16)
            back_core(u).start()
            carried[:, at] = jnp.where(core == 0, entry, later).astype(BF16)

    turn = jnp.minimum(2 + (3 * z + 1) // 2, 7)
    back = jnp.where(z < 2, turn + 2, turn + 1)
    ready = back + 1
    units = pairs // 2
    lights = jnp.where(row == 1, share, below)

    free = is_row0 & (z == 0)

    def light_range(j):
        count = jnp.where(j <= share, 2, 1)
        count = jnp.where((j >= 1) & (j <= slots), count, 0)
        first = jnp.clip(j - 3, 0, lights)
        last = jnp.clip(j - 2, 0, lights)
        return jnp.where(free, 0, first), jnp.where(free, count, last)

    lax.fori_loop(0, pairs, local_state, 0, unroll=4)
    for u in range(2):
        to_core(u).start()
    for one in loads[6:]:
        one.wait()

    def step(j, carry):
        @pl.when(j == turn)
        def _():
            pass_state()

        @pl.when(j < slots - 1)
        def _():
            z_arrived(j, halves)

        @pl.when(j == slots - 1)
        def _():
            z_arrived(slots - 1, pieces)

        @pl.when(j == 0)
        def _():
            chip_totals()
            z_offer(1 + shift, halves)
            side_offer(1)

        @pl.when((j >= 1) & (j <= slots))
        def _():
            @pl.when(j - 1 + shift < slots)
            def _():
                z_sent(j - 1 + shift)

            @pl.when((row == 0) | (j - 1 < served))
            def _():
                y_all(j - 1).wait_send()

        @pl.when(j + 3 + shift < slots)
        def _():
            z_offer(j + 2 + shift, halves)

        @pl.when(j + 3 + shift == slots)
        def _():
            z_offer(slots - 1, pieces)

        @pl.when(j + 2 < slots)
        def _():
            side_offer(j + 2)

        @pl.when((j >= 2) & (j < slots + 2))
        def _():
            a_all(j - 2).wait_recv()
            third_part(j - 2)

        @pl.when((j >= 1) & (j <= slots))
        def _():
            t = j - 1

            @pl.when((t < share) | ((core == 0) & (t < swapped)))
            def _():
                b_all(t).wait_recv()

            @pl.when((core == 1) | (has_z & (share + t >= below)))
            def _():
                b_all(share + t).wait_recv()

            @pl.when(t < share)
            def _():
                serve_early(t)

            first_part(t)
            y_all(t).wait_recv()
            a_all(t).start()
            second_part(t)

        def light(i, carry):
            waiting = jnp.where(i == 0, share + j - 1, j - 1)
            return light_head(jnp.where(free, waiting, i), carry)

        lax.fori_loop(*light_range(j), light, 0)

        @pl.when(j == back)
        def _():
            pass_core()

        @pl.when(j < 4)
        def _():
            for n in range(pairs // 4):
                intra(pairs // 4 * j + n, 0)

        @pl.when(j == ready)
        def _():
            for u in range(2):
                back_core(u).wait_recv()

        def finish_two(n, carry):
            finish(2 * n, carry)
            return finish(2 * n + 1, carry)

        first = jnp.clip(3 * (j - ready), 0, units)
        lax.fori_loop(first, jnp.clip(3 * (j - ready + 1), 0, units), finish_two, 0)

        return carry

    lax.fori_loop(0, slots + 3, step, 0)

    for d in range(1, 4):
        own_dl(d).wait_send()
    for u in range(2):
        to_core(u).wait_send()
        back_core(u).wait_send()
    to_row().wait_send()

    @pl.when(has_z | is_row0)
    def _():
        back_row().wait_send()

    @pl.when(has_next)
    def _():
        to_next().wait_send()

    copy(
        held.at[Y, pl.ds(0, slots)], held.at[A, pl.ds(0, slots)], a_send, a_recv.at[0], beside(1)
    ).wait_send()

    def left(ref, sender):
        copy(ref, ref, sender, up_q_recv.at[0], beside(1)).wait_send()

    def drain(g, carry):
        some = pl.ds(g * share, share)

        @pl.when((core == 0) | (g * share < swapped) | (has_z & (g * share >= below)))
        def _():
            left(held.at[B, some], b_send.at[g])

        @pl.when(has_z & (g * share < below))
        def _():
            left(up_q.at[some], up_q_send.at[g])

        @pl.when(has_next & (g * share < above))
        def _():
            left(down_o.at[some], down_send.at[g, 0])
            left(down_s.at[some], down_send.at[g, 1])

        @pl.when((g * share < slots) & (row == 1) & (g * share >= served))
        def _():
            left(held.at[Y, some], y_relay_send.at[g])

        return carry

    lax.fori_loop(0, nz, drain, 0)

    @pl.when(row == 1)
    def _():
        left(row_q, row_q_send)

    @pl.when(row == 0)
    def _():
        left(back_o, back_send.at[0])
        left(back_s, back_send.at[1])


def on_device(queries, keys, values, ssd_input, bmat, cmat, expo, rate, skip):
    length, total_cols = queries.shape
    size = lax.axis_size("seq")
    head_count = rate.shape[0]
    x_cols = ssd_input.shape[1]
    state = cmat.shape[1]
    heads = total_cols // E
    blocks = length // Q
    group = x_cols // 4
    share = heads // (size // 4)
    slots = heads - share
    vmem = pl.BlockSpec(memory_space=pltpu.VMEM)
    dma = pltpu.SemaphoreType.DMA
    inputs = (
        queries, keys, values, ssd_input, bmat, cmat, expo.T, rate[None, :], skip[None, :]
    )
    big = [pltpu.VMEM(a.shape, a.dtype) for a in inputs]
    return pl.pallas_call(
        functools.partial(kernel, size),
        in_specs=[pl.BlockSpec(memory_space=pltpu.HBM)] * len(inputs),
        out_specs=(vmem, vmem),
        out_shape=(
            jax.ShapeDtypeStruct(queries.shape, BF16),
            jax.ShapeDtypeStruct(ssd_input.shape, BF16),
        ),
        scratch_shapes=[
            *big,
            pltpu.VMEM((4, heads, 2, length, E), BF16),
            pltpu.VMEM((LANES, x_cols), BF16),
            pltpu.VMEM((length, LANES), BF16),
            pltpu.VMEM((head_count, length), F32),
            pltpu.VMEM((state, length), BF16),
            pltpu.VMEM((blocks, Q, Q), F32),
            pltpu.VMEM((8, x_cols), F32),
            pltpu.VMEM((8, x_cols), F32),
            pltpu.VMEM((4, 8, LANES), F32),
            pltpu.VMEM((8, x_cols), F32),
            pltpu.VMEM((blocks, state, x_cols), F32),
            pltpu.VMEM((state, x_cols), BF16),
            pltpu.VMEM((2, state, group), BF16),
            pltpu.VMEM((2, state, group), BF16),
            pltpu.VMEM((state, group), BF16),
            pltpu.VMEM((state, group), BF16),
            pltpu.VMEM((state, group), BF16),
            pltpu.VMEM((state, group), BF16),
            pltpu.VMEM((2, state, group), BF16),
            pltpu.VMEM((2, state, group), BF16),
            pltpu.VMEM((state, x_cols), BF16),
            pltpu.VMEM((length, x_cols), F32),
            pltpu.VMEM((2, length, E), F32),
            pltpu.VMEM((2, 2, length, E), F32),
            pltpu.VMEM((length, E), BF16),
            pltpu.VMEM((heads, length, E), BF16),
            pltpu.VMEM((heads, length, E), BF16),
            pltpu.VMEM((heads, 8, length), F32),
            pltpu.VMEM((heads, length, E), BF16),
            pltpu.VMEM((heads, 8, length), F32),
            pltpu.VMEM((share, length, E), BF16),
            pltpu.VMEM((share, length, E), BF16),
            pltpu.VMEM((share, 8, length), F32),
            pltpu.VMEM((share, length, E), BF16),
            pltpu.VMEM((share, 8, length), F32),
            dma((9,)),
            dma((slots,)),
            dma((slots, 2)),
            dma((8,)),
            dma((slots,)),
            dma((slots,)),
            dma,
            dma((slots,)),
            dma((heads // share,)),
            dma((heads,)),
            dma((heads // share,)),
            dma((heads // share,)),
            dma((heads,)),
            dma((heads // share, 2)),
            dma((heads, 2)),
            dma,
            dma((share,)),
            dma((2,)),
            dma((share, 2)),
            dma((4,)),
            dma((4,)),
            dma((2,)),
            dma((2,)),
            dma((2,)),
            dma((2,)),
            dma((3,)),
            dma((3,)),
        ],
        compiler_params=pltpu.CompilerParams(
            collective_id=0, has_side_effects=True, vmem_limit_bytes=48 << 20
        ),
        name="attention_and_recurrence",
    )(*(pltpu.with_memory_space_constraint(a, pltpu.HBM) for a in inputs))


def solution(mesh):
    split_rows = P(("groups", "seq"), None)
    return jax.shard_map(
        on_device,
        mesh=mesh,
        in_specs=(split_rows,) * 7 + (P(), P()),
        out_specs=(split_rows, split_rows),
        check_vma=False,
    )
```

```python
import functools
import math

import jax
import jax.numpy as jnp
from jax import lax
from jax.experimental import pallas as pl
from jax.experimental.pallas import tpu as pltpu
from jax.sharding import PartitionSpec as P

E = 128
Q = 256
LANES = 128
NEG = -1e30
LOG2E = math.log2(math.e)
MESH = pl.DeviceIdType.MESH
Z, Y, A, B = range(4)
BF16 = jnp.bfloat16
F32 = jnp.float32


def dot(a, b):
    return jnp.dot(a, b, preferred_element_type=F32)


def dot_t(a, b):
    return lax.dot_general(a, b, (((1,), (1,)), ((), ())), preferred_element_type=F32)


def iota(shape, axis):
    return lax.broadcasted_iota(jnp.int32, shape, axis)


def split(a):
    high = a.astype(BF16)
    rest = a - high.astype(F32)
    middle = rest.astype(BF16)
    return high, middle, (rest - middle.astype(F32)).astype(BF16)


def table(a):
    parts = split(a)
    rest = jnp.zeros((a.shape[0], LANES - 3 * a.shape[1]), BF16)
    return jnp.concatenate([*parts, rest], axis=1)


def wide(a):
    return jnp.concatenate([a, jnp.zeros((a.shape[0], LANES - a.shape[1]), F32)], axis=1)


def lanes_of(j):
    return pl.ds(pl.multiple_of(j * LANES, LANES), LANES)


def flash(q, tiles, m, l, acc):
    tq = q.shape[0]
    scale = LOG2E / math.sqrt(E)
    for k, v, mask in tiles:
        s = dot_t(q, k) * scale
        if mask is not None:
            row, col = iota((tq, tq), 0), iota((tq, tq), 1)
            s = jnp.where(col <= row if mask == "low" else col > row, s, NEG)
        groups = s.shape[1] // LANES
        peak = jnp.broadcast_to(jnp.max(s, axis=1, keepdims=True), (tq, LANES))
        m_new = peak if m is None else jnp.maximum(m, peak)
        p = jnp.exp2(s - jnp.concatenate([m_new] * groups, axis=1))
        total = p[:, 0:LANES]
        for g in range(1, groups):
            total = total + p[:, g * LANES : (g + 1) * LANES]
        part = dot(p.astype(BF16), v)
        if m is None:
            l, acc = total, part
        else:
            alpha = jnp.exp2(m - m_new)
            l = l * alpha + total
            acc = acc * alpha + part
        m = m_new
    return m, l, acc


def attend(q, tiles):
    tq = q.shape[0]
    scale = LOG2E / math.sqrt(E)
    low = iota((tq, tq), 1) <= iota((tq, tq), 0)
    scores = []
    for k, v, mask in tiles:
        s = dot_t(q, k) * scale
        if isinstance(mask, tuple):
            s = jnp.where(low, s, dot_t(q, mask[0]) * scale)
        elif mask is not None:
            s = jnp.where(low, s, NEG) if mask == "low" else jnp.where(low, NEG, s)
        scores.append(s)
    peak = functools.reduce(jnp.maximum, [jnp.max(s, axis=1, keepdims=True) for s in scores])
    m = jnp.broadcast_to(peak, (tq, LANES))
    l = acc = 0.0
    for s, (k, v, mask) in zip(scores, tiles):
        groups = s.shape[1] // LANES
        p = jnp.exp2(s - jnp.concatenate([m] * groups, axis=1))
        for g in range(groups):
            l = l + p[:, g * LANES : (g + 1) * LANES]
        if isinstance(mask, tuple):
            acc = acc + dot(jnp.where(low, p, 0.0).astype(BF16), v)
            acc = acc + dot(jnp.where(low, 0.0, p).astype(BF16), mask[1])
        else:
            acc = acc + dot(p.astype(BF16), v)
    return m, l, acc


def whole_sum(l):
    return jnp.sum(l, axis=1, keepdims=True)


def kernel(
    size, q_in, k_in, v_in, x_in, b_in, c_in, expo_in, rate_in, skip_in, attn_ref, rec_ref,
    q_ref, k_ref, v_ref, x_ref, b_ref, c_ref, expo_ref, rate_ref, skip_ref, held, hot, t3, cumt, bt,
    cross, dec, skx, dl, dtab, local, tot, s1, tc, s2, ein, eout, s4out, ec, s5out, carried, mixed,
    acc_ref, ml_ref, q_now, up_q, up_o, up_s, down_o, down_s, row_q, row_o, row_s, back_o, back_s,
    load, z_send, z_recv, last_recv, y_send, y_recv, a_send, a_recv, b_send, b_recv,
    y_relay_send, up_q_send, up_q_recv, down_send, down_recv, row_q_send, row_q_recv, back_send, back_recv,
    dl_send, dl_recv, s1_send, s1_recv, s5_send, s5_recv, one_send, one_recv,
):
    nz = size // 4
    here = lax.axis_index("seq")
    mine = lax.axis_index("groups")
    z = here // 4
    member = here % 4
    row = member // 2
    core = member % 2
    length, total_cols = q_ref.shape
    x_cols = x_ref.shape[1]
    heads = total_cols // E
    pairs = x_cols // LANES
    head_count = rate_ref.shape[1]
    width = x_cols // head_count
    group = x_cols // 4
    blocks = length // Q
    tq = min(256, length)
    has_z = z > 0
    has_next = z < nz - 1
    assert heads % nz == 0
    share = heads // nz
    slots = heads - share
    served = share * (nz - 1 - z)
    is_row0 = row == 0
    below = jnp.where(is_row0 | (z == 0), share * (nz - z), share)
    above = jnp.where(is_row0, served, jnp.where(has_next, share, 0))
    swapped = jnp.maximum(above, share)

    def beside(d):
        r = 1 - row if d // 2 else row
        c = 1 - core if d % 2 else core
        return (mine, z * 4 + 2 * r + c)

    def beyond(step):
        return (mine, (z + step + nz) % nz * 4 + member)

    def copy(src, dst, sender, receiver, device):
        return pltpu.make_async_remote_copy(
            src_ref=src, dst_ref=dst, send_sem=sender, recv_sem=receiver,
            device_id=device, device_id_type=MESH,
        )

    inputs = (
        (rate_in, rate_ref), (expo_in, expo_ref), (skip_in, skip_ref), (b_in, b_ref), (c_in, c_ref),
        (x_in, x_ref), (q_in, q_ref), (k_in, k_ref), (v_in, v_ref),
    )
    loads = [pltpu.make_async_copy(a, b, load.at[i]) for i, (a, b) in enumerate(inputs)]
    for one in loads[:6]:
        one.start()

    barrier = pltpu.get_barrier_semaphore()
    for d in range(1, 4):
        pl.semaphore_signal(barrier, inc=1, device_id=beside(d), device_id_type=MESH)

    @pl.when(has_z)
    def _():
        pl.semaphore_signal(barrier, inc=1, device_id=beyond(-1), device_id_type=MESH)

    @pl.when(has_next)
    def _():
        pl.semaphore_signal(barrier, inc=1, device_id=beyond(1), device_id_type=MESH)

    pl.semaphore_wait(barrier, 3 + jnp.minimum(z, 1) + jnp.minimum(nz - 1 - z, 1))

    def team(h):
        return lax.div(h, share)

    halves = [(part, slice(0, length)) for part in range(2)]
    piece = length // 4
    pieces = [(part, slice(i * piece, (i + 1) * piece)) for part in range(2) for i in range(4)]

    def y_head(t, to):
        return jnp.where((to == 0) & (t < served), t, share + t)

    def z_copy(t, n, cut):
        part, rows = cut[n]
        h = share + t
        arrival = z_recv.at[t, n] if cut is halves else last_recv.at[n]
        return copy(
            (k_in, v_in)[part].at[rows, lanes_of(h)], held.at[Z, h, part, rows], z_send.at[t],
            arrival, beyond(1),
        )

    def z_arrived(t, cut):
        h = share + t

        @pl.when(has_z & (h >= below))
        def _():
            for n, (part, rows) in enumerate(cut):
                z_copy(t, n, cut).wait_recv()

                @pl.when((row == 1) & (t >= served))
                def _():
                    copy(
                        held.at[Z, h, part, rows], held.at[Y, h, part, rows],
                        y_relay_send.at[team(t)], y_recv.at[t], beside(2),
                    ).start()

                @pl.when(core == 1)
                def _():
                    copy(
                        held.at[Z, h, part, rows], held.at[B, h, part, rows], b_send.at[team(h)],
                        b_recv.at[h], beside(1),
                    ).start()

    def z_sent(t):
        @pl.when(has_next & (share + t >= above))
        def _():
            copy(
                held.at[Z, share + t], held.at[Z, share + t], z_send.at[t], z_recv.at[0, 0], beyond(1)
            ).wait_send()

    def z_offer(t, cut):
        @pl.when(has_next & (share + t >= above))
        def _():
            for n in range(len(cut)):
                z_copy(t, n, cut).start()

    def y_all(t):
        h = y_head(t, row)
        return copy(held.at[Y, h], held.at[Y, h], y_send.at[t], y_recv.at[t], beside(2))

    def a_all(t):
        h = y_head(t, row)
        return copy(held.at[Y, h], held.at[A, h], a_send, a_recv.at[t], beside(1))

    def b_all(h):
        return copy(held.at[B, h], held.at[B, h], b_send.at[0], b_recv.at[h], beside(1))

    def b_own(h):
        for part, ref in ((0, k_in), (1, v_in)):
            copy(
                ref.at[:, lanes_of(h)], held.at[B, h, part], b_send.at[team(h)], b_recv.at[h],
                beside(1),
            ).start()

    def to_below(h):
        return copy(
            q_in.at[:, lanes_of(h)], up_q.at[h], up_q_send.at[team(h)], up_q_recv.at[h], beyond(-1)
        )

    def to_above(h):
        return (
            copy(down_o.at[h], up_o.at[h], down_send.at[team(h), 0], down_recv.at[h, 0], beyond(1)),
            copy(down_s.at[h], up_s.at[h], down_send.at[team(h), 1], down_recv.at[h, 1], beyond(1)),
        )

    def ask_row(h):
        return copy(
            q_in.at[:, lanes_of(h)], row_q.at[h], row_q_send, row_q_recv.at[h], beside(2)
        )

    def answer_row(h):
        return (
            copy(back_o.at[h], row_o.at[h], back_send.at[0], back_recv.at[h, 0], beside(2)),
            copy(back_s.at[h], row_s.at[h], back_send.at[1], back_recv.at[h, 1], beside(2)),
        )

    def side_offer(t):
        @pl.when((row == 1) & (t < share))
        def _():
            ask_row(t).start()

        @pl.when((row == 0) | (t < served))
        def _():
            h = y_head(t, 1 - row)
            for part, ref in ((0, k_in), (1, v_in)):
                copy(
                    ref.at[:, lanes_of(h)], held.at[Y, h, part], y_send.at[t], y_recv.at[t],
                    beside(2),
                ).start()

        @pl.when(core == 0)
        def _():
            b_own(share + t)

        @pl.when(((core == 0) & (t < share)) | ((core == 1) & (t < swapped)))
        def _():
            b_own(t)

    shift = jnp.where(has_next, above - share, 0)
    z_offer(shift, halves)
    side_offer(0)

    @pl.when(has_z)
    def _():
        def ask(h, carry):
            to_below(h).start()
            return carry

        lax.fori_loop(0, below, ask, 0)

    for one in loads[6:]:
        one.start()

    def own_dl(d):
        return copy(dl.at[0], dl.at[d], dl_send.at[d], dl_recv.at[d], beside(d))

    def quarter(u, c):
        return pl.ds(pl.multiple_of((2 * u + c) * group, group), group)

    def to_core(u):
        return copy(
            tot.at[:, quarter(u, 1 - core)], s1.at[u], s1_send.at[u], s1_recv.at[u], beside(1)
        )

    def to_row():
        return copy(tc.at[1 - row], s2, one_send.at[0], one_recv.at[0], beside(2))

    def to_next():
        return copy(eout, ein, one_send.at[1], one_recv.at[1], beyond(1))

    def back_row():
        return copy(s4out, ec.at[row], one_send.at[2], one_recv.at[2], beside(2))

    def back_core(u):
        return copy(
            s5out.at[u], carried.at[:, quarter(u, core)], s5_send.at[u], s5_recv.at[u], beside(1)
        )

    ki = iota((LANES, x_cols), 0)
    hi = lax.div(iota((LANES, x_cols), 1), width)
    match = ki == hi
    for p in (1, 2):
        match = match | (ki - p * head_count == hi)
    hot[...] = jnp.where(match, 1.0, 0.0).astype(BF16)

    @pl.when(z == 0)
    def _():
        ein[...] = jnp.zeros_like(ein)

    low = iota((Q, Q), 1) <= iota((Q, Q), 0)
    upto = jnp.where(iota((Q, Q), 0) <= iota((Q, Q), 1), 1.0, 0.0).astype(BF16)
    loads[0].wait()
    loads[1].wait()
    rates = wide(rate_ref[...])[0:1, :]
    rates = jnp.broadcast_to(rates, (LANES, LANES)).T[0:head_count, 0:1]
    dlog = None
    for b in range(blocks):
        rs = slice(b * Q, (b + 1) * Q)
        loga = -rates * expo_ref[:, rs].astype(F32)
        sums = sum(dot(part, upto) for part in split(loga))
        cumt[:, rs] = sums
        rest = jnp.zeros((LANES - head_count, Q), F32)
        cum = jnp.concatenate([sums, rest], axis=0).T[:, 0:head_count]
        t3[rs, :] = table(cum)
        last = cum[Q - 1 :, :]
        dlog = last if dlog is None else dlog + last
    dl[0] = jnp.broadcast_to(wide(dlog), dl.shape[1:])
    for d in range(1, 4):
        own_dl(d).start()
    loads[2].wait()
    skx[...] = jnp.broadcast_to(dot(table(skip_ref[...]), hot[...]), skx.shape)
    loads[3].wait()
    loads[4].wait()
    bt[...] = b_ref[...].astype(F32).T.astype(BF16)
    for b in range(blocks):
        rs = slice(b * Q, (b + 1) * Q)
        cross[b] = jnp.where(low, dot_t(c_ref[rs, :], b_ref[rs, :]), 0.0)
    loads[5].wait()

    lane = iota((1, LANES), 1)

    def spread(rs, cs):
        return dot(t3[rs, :], hot[:, cs])

    def local_state(j, carry):
        cs = lanes_of(j)
        state = None
        for b in range(blocks):
            rs = slice(b * Q, (b + 1) * Q)
            cum = spread(rs, cs)
            end = cum[Q - 1 :, :]
            xs = x_ref[rs, cs].astype(F32) * jnp.exp(end - cum)
            one = dot(bt[:, rs], xs.astype(BF16))
            grown = jnp.exp(end)
            local[b, :, cs] = one
            dec[b : b + 1, cs] = grown
            state = one if state is None else state * grown + one
        tot[:, cs] = state.astype(BF16)
        return carry

    def intra(j, carry):
        cs = lanes_of(j)
        for b in range(blocks):
            rs = slice(b * Q, (b + 1) * Q)
            cum = spread(rs, cs)
            x = x_ref[rs, cs]
            both = []
            for a in range(2):
                gap = cum[:, a * width : a * width + 1] - cumt[pl.ds(2 * j + a, 1), rs]
                grid = jnp.exp(jnp.minimum(gap, 0.0))
                both.append(dot((cross[b] * grid).astype(BF16), x))
            mixed[rs, cs] = (
                jnp.where(lane < width, both[0], both[1]) + skx[0:1, cs] * x.astype(F32)
            )
        return carry

    same = (iota((LANES, LANES), 0) < width) == (iota((LANES, LANES), 1) < width)
    ones = jnp.where(same, 1.0, 0.0).astype(BF16)

    def finish(j, carry):
        cs = lanes_of(j)
        entry = carried[:, cs].astype(F32)
        for b in range(blocks):
            rs = slice(b * Q, (b + 1) * Q)
            c = c_ref[rs, :]
            high = entry.astype(BF16)
            inter = dot(c, high)
            if b:
                inter = inter + dot(c, (entry - high.astype(F32)).astype(BF16))
            value = mixed[rs, cs] + inter * jnp.exp(spread(rs, cs))
            square = value * value
            big = square.astype(BF16)
            small = (square - big.astype(F32)).astype(BF16)
            mean = (dot(big, ones) + dot(small, ones)) * (1.0 / width)
            rec_ref[rs, cs] = (value * lax.rsqrt(mean + 1e-05)).astype(rec_ref.dtype)
            if b + 1 < blocks:
                entry = entry * dec[b : b + 1, cs] + local[b, :, cs]
        return carry

    query_rows = [slice(r, r + tq) for r in range(0, length, tq)]

    def keep(slot, rows, m, l, acc):
        acc_ref[slot, rows, :] = acc
        ml_ref[slot, 0, rows, :] = m
        ml_ref[slot, 1, rows, :] = l

    def kept(slot, rows):
        return ml_ref[slot, 0, rows, :], ml_ref[slot, 1, rows, :], acc_ref[slot, rows, :]

    def held_tile(kind, h):
        return (held[kind, h, 0], held[kind, h, 1], None)

    def own_low(h, rows):
        hs = lanes_of(h)
        tiles = [(k_ref[rows, hs], v_ref[rows, hs], "low")]
        if rows.start > 0:
            tiles.append((k_ref[0 : rows.start, hs], v_ref[0 : rows.start, hs], None))
        return tiles

    def own_up(h, rows):
        hs = lanes_of(h)
        tiles = [(k_ref[rows, hs], v_ref[rows, hs], "up")]
        if rows.stop < length:
            tiles.append((k_ref[rows.stop : length, hs], v_ref[rows.stop : length, hs], None))
        return tiles

    def own_and_z(h, rows):
        hs = lanes_of(h)
        z_k, z_v = held[Z, h, 0, rows, :], held[Z, h, 1, rows, :]
        tiles = [(k_ref[rows, hs], v_ref[rows, hs], (z_k, z_v))]
        if rows.start > 0:
            tiles.append((k_ref[0 : rows.start, hs], v_ref[0 : rows.start, hs], None))
        if rows.stop < length:
            past = slice(rows.stop, length)
            tiles.append((held[Z, h, 0, past, :], held[Z, h, 1, past, :], None))
        return tiles

    def begin(slot, q_of, tiles_of):
        for rows in query_rows:
            keep(slot, rows, *attend(q_of(rows), tiles_of(rows)))

    def emit(m, l, acc, o_ref, s_ref, h, rows):
        l = whole_sum(l)
        o_ref[h, rows, :] = (acc / l).astype(BF16)
        top = m + jnp.log(l) * LOG2E
        s_ref[h, :, rows] = top.T[0:8, :]

    def merge(slot, o_ref, s_ref, h):
        for rows in [slice(0, length)]:
            m, l, acc = kept(slot, rows)
            top = jnp.concatenate([s_ref[h, :, rows]] * (LANES // 8), axis=0).T
            m_new = jnp.maximum(m, top)
            mine_part, their_part = jnp.exp2(m - m_new), jnp.exp2(top - m_new)
            keep(
                slot, rows, m_new, l * mine_part + jnp.where(lane == 0, their_part, 0.0),
                acc * mine_part + o_ref[h, rows, :].astype(F32) * their_part,
            )

    def finish_head(slot, h):
        for rows in [slice(0, length)]:
            m, l, acc = kept(slot, rows)
            attn_ref[rows, lanes_of(h)] = (acc / whole_sum(l)).astype(attn_ref.dtype)

    def extend(slot, q, tile):
        rows = slice(0, length)
        keep(slot, rows, *flash(q, [tile], *kept(slot, rows)))

    def own_begin(slot, h):
        hs = lanes_of(h)
        begin(slot, lambda rows: q_ref[rows, hs], lambda rows: own_low(h, rows))

        @pl.when(core == 1)
        def _():
            extend(slot, q_ref[:, hs], held_tile(B, h))

    def serving(t):
        return is_row0 & (t < served)

    def first_part(t):
        @pl.when(serving(t))
        def _():
            to_below(t).wait_recv()
            q_now[...] = up_q[t]

            begin(0, lambda rows: up_q[t, rows, :], lambda rows: own_up(t, rows))

            @pl.when(core == 0)
            def _():
                extend(0, up_q[t], held_tile(B, t))

        @pl.when(jnp.logical_not(serving(t)))
        def _():
            h = share + t
            q_now[...] = q_ref[:, lanes_of(h)]

            @pl.when(has_z)
            def _():
                begin(
                    0, lambda rows: q_ref[rows, lanes_of(h)],
                    lambda rows: own_and_z(h, rows),
                )
                extend(0, q_ref[:, lanes_of(h)], held_tile(B, h))

            @pl.when(z == 0)
            def _():
                own_begin(0, h)

    def second_part(t):
        h = y_head(t, row)
        rows = slice(0, length)
        keep(0, rows, *flash(q_now[rows, :], [held_tile(Y, h)], *kept(0, rows)))

    def third_part(t):
        h = y_head(t, row)
        rows = slice(0, length)
        keep(0, rows, *flash(q_now[rows, :], [held_tile(A, h)], *kept(0, rows)))

        @pl.when(serving(t))
        def _():
            for rows in [slice(0, length)]:
                emit(*kept(0, rows), down_o, down_s, t, rows)
            for one in to_above(t):
                one.start()

        @pl.when(jnp.logical_not(serving(t)))
        def _():
            finish_head(0, h)

    def serve_early(h):
        @pl.when(is_row0)
        def _():
            ask_row(h).wait_recv()
            hs = lanes_of(h)
            own = (k_ref[:, hs], v_ref[:, hs], None)
            result = flash(row_q[h], [own, held_tile(B, h)], None, None, None)
            emit(*result, back_o, back_s, h, slice(0, length))
            for one in answer_row(h):
                one.start()

        @pl.when((row == 1) & has_next)
        def _():
            to_below(h).wait_recv()

            begin(1, lambda rows: up_q[h, rows, :], lambda rows: own_up(h, rows))

            @pl.when(core == 0)
            def _():
                extend(1, up_q[h], held_tile(B, h))

            for rows in [slice(0, length)]:
                emit(*kept(1, rows), down_o, down_s, h, rows)
            for one in to_above(h):
                one.start()

    def light_head(h, carry):
        own_begin(1, h)

        @pl.when(row == 1)
        def _():
            for one in answer_row(h):
                one.wait_recv()
            merge(1, row_o, row_s, h)

        @pl.when(has_z)
        def _():
            for one in to_above(h):
                one.wait_recv()
            merge(1, up_o, up_s, h)

        finish_head(1, h)
        return carry

    def decays(*which):
        for d in which:
            if d:
                own_dl(d).wait_recv()
        line = iota((8, LANES), 0)
        rows = sum(jnp.where(line == i, dl[d], 0.0) for i, d in enumerate(which))
        spread_out = jnp.exp(dot(table(rows[:, :head_count]), hot[...]))
        dtab[which[0] : which[0] + 2, :] = spread_out[0:2, :]

    def chip_totals():
        decays(0, 1)
        for u in range(2):
            to_core(u).wait_recv()
            at = quarter(u, core)
            theirs = jnp.where(core == 1, dtab[0:1, at], 1.0)
            ours = jnp.where(core == 1, 1.0, dtab[1:2, at])
            tc[u] = (theirs * s1[u].astype(F32) + ours * tot[:, at].astype(F32)).astype(BF16)
        to_row().start()

    def pass_state():
        decays(2, 3)
        to_row().wait_recv()

        @pl.when(has_z)
        def _():
            to_next().wait_recv()

        at = quarter(row, core)
        near = dtab[0:1, at] * dtab[1:2, at]
        far = dtab[2:3, at] * dtab[3:4, at]
        entry = ein[...].astype(F32)
        ours, theirs = tc[row].astype(F32), s2[...].astype(F32)
        quad = jnp.where(row == 1, near, 1.0) * theirs + jnp.where(row == 1, 1.0, far) * ours

        @pl.when(has_next)
        def _():
            eout[...] = (near * far * entry + quad).astype(BF16)
            to_next().start()

        @pl.when(has_z | is_row0)
        def _():
            s4out[...] = jnp.where(row == 0, near * entry + ours, entry).astype(BF16)
            back_row().start()

        @pl.when((z == 0) & is_row0)
        def _():
            ec[1] = jnp.zeros(ec.shape[1:], BF16)

        ec[row] = jnp.where(row == 0, entry, far * entry + theirs).astype(BF16)

    def pass_core():
        @pl.when(has_z | (row == 1))
        def _():
            back_row().wait_recv()

        for u in range(2):
            at = quarter(u, core)
            entry = ec[u].astype(F32)
            later = jnp.where(core == 0, dtab[0:1, at], dtab[1:2, at]) * entry
            later = later + jnp.where(core == 0, tot[:, at], s1[u]).astype(F32)
            s5out[u] = jnp.where(core == 0, later, entry).astype(BF16)
            back_core(u).start()
            carried[:, at] = jnp.where(core == 0, entry, later).astype(BF16)

    turn = jnp.minimum(2 + (3 * z + 1) // 2, 7)
    back = jnp.where(z < 2, turn + 2, turn + 1)
    ready = back + 1
    units = pairs // 2
    lights = jnp.where(row == 1, share, below)
    lag = 3

    def light_count(j):
        soon = jnp.where(j > slots // 2 + 2, j - 2, j - 3)
        return jnp.clip(jnp.where(is_row0 & (z == 1), soon, j - lag), 0, lights)


    free = is_row0 & (z == 0)

    def light_range(j):
        count = jnp.where(j <= share, 2, 1)
        count = jnp.where((j >= 1) & (j <= slots), count, 0)
        first, last = light_count(j), light_count(j + 1)
        return jnp.where(free, 0, first), jnp.where(free, count, last)

    lax.fori_loop(0, pairs, local_state, 0, unroll=4)
    for u in range(2):
        to_core(u).start()
    for one in loads[6:]:
        one.wait()

    def left(ref, sender):
        copy(ref, ref, sender, up_q_recv.at[0], beside(1)).wait_send()

    def drain_early():
        for d in range(1, 4):
            own_dl(d).wait_send()
        for u in range(2):
            to_core(u).wait_send()
        to_row().wait_send()
        for g in range(nz):

            @pl.when(has_z & (g * share < below))
            def _():
                left(up_q.at[g * share : (g + 1) * share], up_q_send.at[g])

        @pl.when(row == 1)
        def _():
            left(row_q, row_q_send)

        @pl.when(row == 0)
        def _():
            left(back_o, back_send.at[0])
            left(back_s, back_send.at[1])

    def step(j, carry):
        @pl.when(j == slots - 2)
        def _():
            drain_early()

        @pl.when(j == turn)
        def _():
            pass_state()

        @pl.when(j < slots - 1)
        def _():
            z_arrived(j, halves)

        @pl.when(j == slots - 1)
        def _():
            z_arrived(slots - 1, pieces)

        @pl.when(j == 0)
        def _():
            chip_totals()
            z_offer(1 + shift, halves)
            side_offer(1)

        @pl.when((j >= 1) & (j <= slots))
        def _():
            @pl.when(j - 1 + shift < slots)
            def _():
                z_sent(j - 1 + shift)

            @pl.when((row == 0) | (j - 1 < served))
            def _():
                y_all(j - 1).wait_send()

        @pl.when(j + 3 + shift < slots)
        def _():
            z_offer(j + 2 + shift, halves)

        @pl.when(j + 3 + shift == slots)
        def _():
            z_offer(slots - 1, pieces)

        @pl.when(j + 2 < slots)
        def _():
            side_offer(j + 2)

        @pl.when((j >= 2) & (j < slots + 2))
        def _():
            a_all(j - 2).wait_recv()
            third_part(j - 2)

        @pl.when((j >= 1) & (j <= slots))
        def _():
            t = j - 1

            @pl.when((t < share) | ((core == 0) & (t < swapped)))
            def _():
                b_all(t).wait_recv()

            @pl.when((core == 1) | (has_z & (share + t >= below)))
            def _():
                b_all(share + t).wait_recv()

            @pl.when(t < share)
            def _():
                serve_early(t)

            first_part(t)
            y_all(t).wait_recv()
            a_all(t).start()
            second_part(t)

        def light(i, carry):
            waiting = jnp.where(i == 0, share + j - 1, j - 1)
            return light_head(jnp.where(free, waiting, i), carry)

        lax.fori_loop(*light_range(j), light, 0)

        @pl.when(j == back)
        def _():
            pass_core()

        @pl.when(j < 4)
        def _():
            for n in range(pairs // 4):
                intra(pairs // 4 * j + n, 0)

        @pl.when(j == ready)
        def _():
            for u in range(2):
                back_core(u).wait_recv()

        def finish_two(n, carry):
            finish(2 * n, carry)
            return finish(2 * n + 1, carry)

        first = jnp.clip(3 * (j - ready), 0, units)
        lax.fori_loop(first, jnp.clip(3 * (j - ready + 1), 0, units), finish_two, 0)

        return carry

    lax.fori_loop(0, slots + 2, step, 0)

    for u in range(2):
        back_core(u).wait_send()

    @pl.when(has_z | is_row0)
    def _():
        back_row().wait_send()

    @pl.when(has_next)
    def _():
        to_next().wait_send()

    copy(
        held.at[Y, pl.ds(0, slots)], held.at[A, pl.ds(0, slots)], a_send, a_recv.at[0], beside(1)
    ).wait_send()

    def drain(g, carry):
        some = pl.ds(g * share, share)

        @pl.when((core == 0) | (g * share < swapped) | (has_z & (g * share >= below)))
        def _():
            left(held.at[B, some], b_send.at[g])

        @pl.when(has_next & (g * share < above))
        def _():
            left(down_o.at[some], down_send.at[g, 0])
            left(down_s.at[some], down_send.at[g, 1])

        @pl.when((g * share < slots) & (row == 1) & (g * share >= served))
        def _():
            left(held.at[Y, some], y_relay_send.at[g])

        return carry

    lax.fori_loop(0, nz, drain, 0)


def on_device(queries, keys, values, ssd_input, bmat, cmat, expo, rate, skip):
    length, total_cols = queries.shape
    size = lax.axis_size("seq")
    head_count = rate.shape[0]
    x_cols = ssd_input.shape[1]
    state = cmat.shape[1]
    heads = total_cols // E
    blocks = length // Q
    group = x_cols // 4
    share = heads // (size // 4)
    slots = heads - share
    vmem = pl.BlockSpec(memory_space=pltpu.VMEM)
    dma = pltpu.SemaphoreType.DMA
    inputs = (
        queries, keys, values, ssd_input, bmat, cmat, expo.T, rate[None, :], skip[None, :]
    )
    big = [pltpu.VMEM(a.shape, a.dtype) for a in inputs]
    return pl.pallas_call(
        functools.partial(kernel, size),
        in_specs=[pl.BlockSpec(memory_space=pltpu.HBM)] * len(inputs),
        out_specs=(vmem, vmem),
        out_shape=(
            jax.ShapeDtypeStruct(queries.shape, BF16),
            jax.ShapeDtypeStruct(ssd_input.shape, BF16),
        ),
        scratch_shapes=[
            *big,
            pltpu.VMEM((4, heads, 2, length, E), BF16),
            pltpu.VMEM((LANES, x_cols), BF16),
            pltpu.VMEM((length, LANES), BF16),
            pltpu.VMEM((head_count, length), F32),
            pltpu.VMEM((state, length), BF16),
            pltpu.VMEM((blocks, Q, Q), F32),
            pltpu.VMEM((8, x_cols), F32),
            pltpu.VMEM((8, x_cols), F32),
            pltpu.VMEM((4, 8, LANES), F32),
            pltpu.VMEM((8, x_cols), F32),
            pltpu.VMEM((blocks, state, x_cols), F32),
            pltpu.VMEM((state, x_cols), BF16),
            pltpu.VMEM((2, state, group), BF16),
            pltpu.VMEM((2, state, group), BF16),
            pltpu.VMEM((state, group), BF16),
            pltpu.VMEM((state, group), BF16),
            pltpu.VMEM((state, group), BF16),
            pltpu.VMEM((state, group), BF16),
            pltpu.VMEM((2, state, group), BF16),
            pltpu.VMEM((2, state, group), BF16),
            pltpu.VMEM((state, x_cols), BF16),
            pltpu.VMEM((length, x_cols), F32),
            pltpu.VMEM((2, length, E), F32),
            pltpu.VMEM((2, 2, length, E), F32),
            pltpu.VMEM((length, E), BF16),
            pltpu.VMEM((heads, length, E), BF16),
            pltpu.VMEM((heads, length, E), BF16),
            pltpu.VMEM((heads, 8, length), F32),
            pltpu.VMEM((heads, length, E), BF16),
            pltpu.VMEM((heads, 8, length), F32),
            pltpu.VMEM((share, length, E), BF16),
            pltpu.VMEM((share, length, E), BF16),
            pltpu.VMEM((share, 8, length), F32),
            pltpu.VMEM((share, length, E), BF16),
            pltpu.VMEM((share, 8, length), F32),
            dma((9,)),
            dma((slots,)),
            dma((slots, 2)),
            dma((8,)),
            dma((slots,)),
            dma((slots,)),
            dma,
            dma((slots,)),
            dma((heads // share,)),
            dma((heads,)),
            dma((heads // share,)),
            dma((heads // share,)),
            dma((heads,)),
            dma((heads // share, 2)),
            dma((heads, 2)),
            dma,
            dma((share,)),
            dma((2,)),
            dma((share, 2)),
            dma((4,)),
            dma((4,)),
            dma((2,)),
            dma((2,)),
            dma((2,)),
            dma((2,)),
            dma((3,)),
            dma((3,)),
        ],
        compiler_params=pltpu.CompilerParams(
            collective_id=0, has_side_effects=True, vmem_limit_bytes=48 << 20
        ),
        name="attention_and_recurrence",
    )(*(pltpu.with_memory_space_constraint(a, pltpu.HBM) for a in inputs))


def solution(mesh):
    split_rows = P(("groups", "seq"), None)
    return jax.shard_map(
        on_device,
        mesh=mesh,
        in_specs=(split_rows,) * 7 + (P(), P()),
        out_specs=(split_rows, split_rows),
        check_vma=False,
    )
```
